1024 devices in a mesh: stretch: 8 (over z_hi, y), head: 2 (over core), blk: 64 (over z_lo, x).
Axes of the slice: x: 4, y: 4, z: 32 (z_hi: 2, z_lo: 16; z = z_hi * 16 + z_lo), core: 2. Of those that a mesh axis runs over, the one named last changes fastest.
Arguments:
- queries: bfloat16 [65536, 3072], P(('stretch', 'blk'), 'head'), may hold values from -200 to 200
- keys: bfloat16 [65536, 512], P(('stretch', 'blk'), 'head'), may hold values from -6 to 6
- values: bfloat16 [65536, 512], P(('stretch', 'blk'), 'head'), may hold values from -24 to 24
- key_norm_gain: float32 [512], P('head'), may hold values from 0.5 to 4
- stretch_ids: int32 [8, 64], P('stretch', 'blk'), may hold values from 0 to 15, never falling along the last dimension, each value on 1 to 8 neighbouring positions
- clean_flags: int32 [8, 64], P('stretch', 'blk'), may hold values 0 or 1
- positions: int32 [8, 64], P('stretch', 'blk'), may hold values from 0 to 2047
Outputs:
- attended: bfloat16 [65536, 3072], P(('stretch', 'blk'), 'head')
The draws below stay inside these ranges and needn't reach their ends.
Inputs may be any that keep to these rules, and one draw needn't show every extreme that they name: `stretch_ids`: stretch numbers start at 0 in each group of 64 blocks and never fall within it; each stretch has 1 to 8 blocks and one stretch of each group has exactly 8.
All inputs are finite; a program needn't handle non-finite values. No bound on the sum of `clean_flags` on one device may be relied on, other than what follows from the above.
Results may differ from the reference program's by a relative error of at most 0.017.
The reference program's roundings to bfloat16 on the way count: a program that leaves them out, or rounds other values in their place, can miss the bound.
Values may be sent and summed in bfloat16 or wider, within the bound.
No kernel may reach another device: no remote copies, remote signals or barrier semaphores. Data moves between devices by JAX's collectives and lax.ppermute only.
A program may use at most 32 MiB of HBM per device.

```python
import math
import jax
import jax.numpy as jnp
import numpy as np
from jax import lax

HEAD_WIDTH = 128
QUERY_HEADS = 24
KEY_VALUE_HEADS = 4
WINDOW_BLOCKS = 3
TOKEN_COUNT = 65536
N_STRETCH = 8
N_BLK = 64


def drawn_key_rows(key):
    clean_portion = jax.random.normal(jax.random.fold_in(key, 11), (TOKEN_COUNT, KEY_VALUE_HEADS * HEAD_WIDTH), jnp.float32)
    return jnp.clip(clean_portion, -6.0, 6.0)


def draw_keys(key, part):
    return drawn_key_rows(key).astype(jnp.bfloat16)


def draw_queries(key, part):
    clean_portion = jnp.clip(jax.random.normal(jax.random.fold_in(key, 21), (TOKEN_COUNT, QUERY_HEADS * HEAD_WIDTH), jnp.float32), -6.0, 6.0)
    return jnp.clip(clean_portion, -200.0, 200.0).astype(jnp.bfloat16)


def place_ends(array, own_key, low, top_value):
    place = [jax.random.randint(jax.random.fold_in(own_key, axis), (), 0, length) for axis, length in enumerate(array.shape)]
    longest = array.shape.index(max(array.shape))
    beside = place[:longest] + [(place[longest] + 1) % array.shape[longest]] + place[longest + 1:]
    return array.at[tuple(place)].set(low).at[tuple(beside)].set(top_value)


def block_scale(stream_key, extent, shards, smallest, top_value):
    def one(dim, blocks):
        steps = jax.random.uniform(jax.random.fold_in(jax.random.fold_in(stream_key, 6), dim), (blocks,), jnp.float32, smallest / len(shards), top_value / len(shards))
        return jnp.repeat(jnp.exp(steps), extent[dim] // blocks).reshape((-1,) + (1,) * (len(extent) - dim - 1))

    factor_of = one(*shards[0])
    for cut in shards[1:]:
        factor_of = factor_of * one(*cut)
    return factor_of


def profile(count, total, most, lean):
    loads = [(1 << 20) // math.isqrt(rank ** lean) + 1 for rank in range(2, count + 1)]
    surplus, given = total - most - (count - 1), [1] * (count - 1)
    while surplus > 0:
        candidates = [i for i in range(count - 1) if given[i] < most]
        pool, remaining = sum([loads[i] for i in candidates]), surplus
        for i in candidates:
            addition = min(most - given[i], max(1, remaining * loads[i] // pool), surplus)
            given[i] = given[i] + addition
            surplus = surplus - addition
    return np.array([most] + given)


def uneven_parts(rng, number_of, total, limit, slope):
    if number_of == 2:
        one = jax.random.randint(rng, (), max(1, total - limit), min(limit, total - 1) + 1)
        return jnp.stack([one, total - one])
    tallies = jnp.asarray(profile(number_of, total, limit, slope), jnp.int32)
    twos = (number_of - 1) // 2
    source_of, sink = tallies[1:1 + 2 * twos:2], tallies[2:2 + 2 * twos:2]
    room = jnp.minimum(source_of - 1, limit - sink)
    passed = jax.random.randint(jax.random.fold_in(rng, 1), (twos,), 0, 1 << 20) % (room + 1)
    tallies = tallies.at[1:1 + 2 * twos:2].set(source_of - passed).at[2:2 + 2 * twos:2].set(sink + passed)
    return tallies[jax.random.permutation(jax.random.fold_in(rng, 2), number_of)]


def centred(stream_key, extent, deviation, bound, split=(), kind=jnp.bfloat16):
    values = deviation * jax.random.normal(stream_key, extent, jnp.float32)
    if split:
        values = values * block_scale(stream_key, extent, split, -0.22, 0.18)
    return jnp.clip(values, -bound, bound).astype(kind)


def setup_inputs(seed: int = 0) -> dict:
    key_of = jax.random.split(jax.random.key(seed), 8)
    return {
        "queries": draw_queries(jax.random.fold_in(key_of[7], 71), 0),
        "keys": draw_keys(jax.random.fold_in(key_of[7], 71), 0),
        "values": centred(key_of[2], (TOKEN_COUNT, KEY_VALUE_HEADS * HEAD_WIDTH), 4.0, 24.0, ((0, 512), (1, 2))),
        "key_norm_gain": jnp.clip(jnp.exp(math.log(4.0) - 2.0794415 * jax.random.uniform(key_of[3], (KEY_VALUE_HEADS * HEAD_WIDTH,), jnp.float32) ** block_scale(key_of[3], (KEY_VALUE_HEADS * HEAD_WIDTH,), ((0, 2),), -0.2, 0.2)), 0.5, 4.0),
        "stretch_ids": jax.vmap(lambda own: jnp.searchsorted(jnp.cumsum(uneven_parts(own, max(1, N_BLK // 4), N_BLK, min(8, N_BLK), 2)), jnp.arange(N_BLK), side="right"))(jax.random.split(key_of[4], N_STRETCH)).reshape((N_STRETCH, N_BLK)).astype(jnp.int32),
        "clean_flags": place_ends((jax.random.randint(key_of[5], (N_STRETCH, N_BLK), 0, 2) < 1).astype(jnp.int32), jax.random.fold_in(key_of[5], 1), 0, 1),
        "positions": place_ends(jax.random.randint(key_of[6], (N_STRETCH, N_BLK), 0, 2048), jax.random.fold_in(key_of[6], 1), 0, 2047).astype(jnp.int32),
    }


ROPE_BASE = 10000.0
NEG_FILL = -1e+30

def apply_rotary_embedding(values_in, positions_f):
    half_dim = values_in.shape[-1] // 2
    frequency = ROPE_BASE ** (-jnp.arange(half_dim, dtype=jnp.float32) * 2.0 / values_in.shape[-1])
    angles = positions_f[:, None, None] * frequency
    cosine = jnp.cos(angles)
    sine_part = jnp.sin(angles)
    first_half = values_in[..., :half_dim]
    second = values_in[..., half_dim:]
    return jnp.concatenate([first_half * cosine - second * sine_part, second * cosine + first_half * sine_part], axis=-1)

def reference(queries, keys, values, key_norm_gain, stretch_ids, clean_flags, positions):
    stretch_count, blk_count = stretch_ids.shape
    block_list = stretch_count * blk_count
    count_of_rows = queries.shape[0] // block_list
    heads_per_group = QUERY_HEADS // KEY_VALUE_HEADS
    score_scale = 1.0 / math.sqrt(HEAD_WIDTH)
    window_span = 2 * WINDOW_BLOCKS + 1
    stretch_global = (stretch_ids + blk_count * jnp.arange(stretch_count, dtype=jnp.int32)[:, None]).astype(jnp.int32).reshape(block_list)
    clean_all = clean_flags.reshape(block_list)
    offsets = jnp.arange(count_of_rows, dtype=jnp.int32)
    token_positions = (positions.reshape(block_list)[:, None] + offsets[None, :]).reshape(-1).astype(jnp.float32)
    unnormed_keys = keys.astype(jnp.float32).reshape(-1, KEY_VALUE_HEADS, HEAD_WIDTH)
    normalized_keys = unnormed_keys * lax.rsqrt(lax.optimization_barrier(jnp.mean(unnormed_keys * unnormed_keys, axis=-1, keepdims=True)) + 1e-06) * key_norm_gain.astype(jnp.float32).reshape(KEY_VALUE_HEADS, HEAD_WIDTH)
    rotated_rows = apply_rotary_embedding(normalized_keys, token_positions).astype(jnp.bfloat16).reshape(block_list, count_of_rows, KEY_VALUE_HEADS, HEAD_WIDTH)
    value_block_rows = values.reshape(block_list, count_of_rows, KEY_VALUE_HEADS, HEAD_WIDTH)
    zero_padding = jnp.zeros((WINDOW_BLOCKS, count_of_rows, KEY_VALUE_HEADS, HEAD_WIDTH), jnp.bfloat16)
    key_padded = jnp.concatenate([zero_padding, rotated_rows, zero_padding], axis=0)
    value_padded = jnp.concatenate([zero_padding, value_block_rows, zero_padding], axis=0)

    def attend_block(block_index):
        query_block_index = lax.dynamic_slice_in_dim(queries, block_index * count_of_rows, count_of_rows, 0).astype(jnp.float32).reshape(count_of_rows, QUERY_HEADS, HEAD_WIDTH)
        query_positions = lax.dynamic_slice_in_dim(token_positions, block_index * count_of_rows, count_of_rows, 0)
        rotated_queries = apply_rotary_embedding(query_block_index, query_positions).astype(jnp.bfloat16).reshape(count_of_rows, KEY_VALUE_HEADS, heads_per_group, HEAD_WIDTH).astype(jnp.float32)
        key_window = lax.dynamic_slice_in_dim(key_padded, block_index, window_span, 0).astype(jnp.float32)
        value_window = lax.dynamic_slice_in_dim(value_padded, block_index, window_span, 0).astype(jnp.float32)
        other_index = block_index - WINDOW_BLOCKS + jnp.arange(window_span, dtype=jnp.int32)
        in_range = (other_index >= 0) & (other_index < block_list)
        safe_index = jnp.clip(other_index, 0, block_list - 1)
        other_stretch = stretch_global[safe_index]
        other_clean = clean_all[safe_index]
        own_stretch = stretch_global[block_index]
        own_clean = clean_all[block_index]
        visible = in_range & ((other_stretch < own_stretch) & (other_clean == 1) | (other_stretch == own_stretch) & (other_clean == own_clean))
        scores = jnp.einsum('qhgd,wkhd->qhgwk', rotated_queries, key_window) * score_scale
        scores = jnp.where(visible[None, None, None, :, None], scores, NEG_FILL)
        best_score = lax.optimization_barrier(jnp.max(scores, axis=(3, 4), keepdims=True))
        weights = jnp.exp(scores - best_score)
        weight_total = lax.optimization_barrier(jnp.sum(weights, axis=(3, 4)))
        rounded = lax.optimization_barrier(weights.astype(jnp.bfloat16)).astype(jnp.float32)
        summed = jnp.einsum('qhgwk,wkhd->qhgd', rounded, value_window)
        attended = summed / weight_total[..., None]
        return attended.reshape(count_of_rows, QUERY_HEADS * HEAD_WIDTH).astype(jnp.bfloat16)
    result = lax.map(attend_block, jnp.arange(block_list, dtype=jnp.int32))
    return result.reshape(block_list * count_of_rows, QUERY_HEADS * HEAD_WIDTH)
```

```python
import math

import jax
import jax.numpy as jnp
import numpy as np
from jax import lax
from jax.experimental import pallas as pl
from jax.experimental.pallas import tpu as pltpu
from jax.sharding import PartitionSpec as P

D = 128
WINDOW = 3
ROPE_BASE = 10000.0
NEG = -1e30
LABEL_ROWS = 16
AXES = ("stretch", "blk")
SCALE = math.log2(math.e) / math.sqrt(D)


def rope_tables(rows):
    half = D // 2
    f = ROPE_BASE ** (-2.0 * np.arange(half) / D)
    f = np.concatenate([f, f])[None, :]
    t = np.arange(rows, dtype=np.float64)[:, None] * f
    a = 128.0 * np.arange(16, dtype=np.float64)[:, None] * f
    cos = np.concatenate([np.cos(t), np.cos(a)], 0)
    sin = np.concatenate([np.sin(t), np.sin(a)], 0)
    return np.stack([cos, sin]).astype(np.float32)


def angles(pos, tab, rows):
    high = lax.shift_right_logical(pos, 7)
    low = lax.bitwise_and(pos, 127)
    ch, sh = tab[0, pl.ds(rows + high, 1), :], tab[1, pl.ds(rows + high, 1), :]
    cl, sl = tab[0, pl.ds(low, 1), :], tab[1, pl.ds(low, 1), :]
    cp = ch * cl - sh * sl
    sp = sh * cl + ch * sl
    ct, st = tab[0, 0:rows, :], tab[1, 0:rows, :]
    lane = lax.broadcasted_iota(jnp.int32, (1, D), 1)
    sign = jnp.where(lane < D // 2, -1.0, 1.0)
    return cp * ct - sp * st, (sp * ct + cp * st) * sign


def rotate(x, cos, sin):
    return x * cos + pltpu.roll(x, D // 2, 1) * sin


def pack_kernel(stretch, clean, pos, k, v, gain, tab, out):
    rows = k.shape[0]
    cos, sin = angles(pos[0, 0], tab, rows)
    for g in range(k.shape[1] // D):
        cols = pl.ds(g * D, D)
        x = k[:, cols].astype(jnp.float32)
        x = x * lax.rsqrt(jnp.mean(x * x, axis=-1, keepdims=True) + 1e-6) * gain[:, cols]
        out[0:rows, cols] = rotate(x, cos, sin).astype(jnp.bfloat16)
    out[pl.ds(rows, rows), :] = v[...]
    label = stretch[0, 0] + 16 * lax.axis_index("stretch")
    row = lax.broadcasted_iota(jnp.int32, (LABEL_ROWS, k.shape[1]), 0)
    info = jnp.where(row == 0, label, jnp.where(row == 1, clean[0, 0], 1))
    out[pl.ds(2 * rows, LABEL_ROWS), :] = info.astype(jnp.float32).astype(jnp.bfloat16)


def labels(ref):
    top = ref.shape[0] - LABEL_ROWS
    info = ref[pl.ds(top, LABEL_ROWS), 0:D].astype(jnp.float32)
    return info[0:1], info[1:2], info[2:3]


def seen(own, other):
    (stretch, clean, _), (stretch2, clean2, there) = own, other
    earlier = (stretch2 < stretch) & (clean2 > 0.5)
    same = (stretch2 == stretch) & (clean2 == clean)
    return (there > 0.5) & (earlier | same)


def scores_of(q, kv, g):
    rows = (kv.shape[0] - LABEL_ROWS) // 2
    keys = kv[0:rows, pl.ds(g * D, D)]
    return lax.dot_general(
        q, keys, (((1,), (1,)), ((), ())), preferred_element_type=jnp.float32
    )


def blend(q, blocks, visible, g, best):
    scores = [scores_of(q, kv, g) for kv in blocks]
    for s, vis in zip(scores, visible):
        top = jnp.where(vis, jnp.max(s, axis=-1, keepdims=True), NEG)
        best = top if best is None else jnp.maximum(best, top)
    shift = best * SCALE
    total, mixed = None, None
    for s, vis, kv in zip(scores, visible, blocks):
        rows = (kv.shape[0] - LABEL_ROWS) // 2
        w = jnp.exp2(s * SCALE - jnp.where(vis, shift, -NEG))
        part = jnp.dot(
            w.astype(jnp.bfloat16),
            kv[pl.ds(rows, rows), pl.ds(g * D, D)],
            preferred_element_type=jnp.float32,
        )
        total = w if total is None else total + w
        mixed = part if mixed is None else mixed + part
    total = jnp.broadcast_to(jnp.sum(total, axis=-1, keepdims=True), best.shape)
    return best, total, mixed


def query_kernel(pos, q, own, tab, rq, again):
    rows, heads = q.shape[0], q.shape[1] // D
    cos, sin = angles(pos[0, 0], tab, rows)
    again[...] = own[...]
    for h in range(heads):
        x = q[:, pl.ds(h * D, D)].astype(jnp.float32)
        rq[pl.ds(h * rows, rows), :] = rotate(x, cos, sin).astype(jnp.bfloat16)


def first_kernel(own, a1, a23, rq, best_out, total_out, mixed_out):
    rows = (own.shape[0] - LABEL_ROWS) // 2
    groups = own.shape[1] // D
    per = rq.shape[0] // rows // groups
    mine = labels(own)
    size = own.shape[0]
    blocks = (own, a1, a23.at[pl.ds(0, size)], a23.at[pl.ds(size, size)])
    visible = [seen(mine, labels(kv)) for kv in blocks]
    for g in range(groups):
        at = pl.ds(g * per * rows, per * rows)
        best, total, mixed = blend(rq[at, :], blocks, visible, g, None)
        best_out[at, :] = best
        total_out[at, :] = total
        mixed_out[at, :] = mixed


def last_kernel(own, b1, b2, b3, rq, best_in, total_in, mixed_in, out):
    rows = out.shape[0]
    groups = own.shape[1] // D
    per = rq.shape[0] // rows // groups
    mine = labels(own)
    blocks = (b3, b2, b1)
    visible = [seen(mine, labels(kv)) for kv in blocks]
    for g in range(groups):
        at = pl.ds(g * per * rows, per * rows)
        before = best_in[at, :]
        best, total, mixed = blend(rq[at, :], blocks, visible, g, before)
        kept = jnp.exp2((before - best) * SCALE)
        total = total_in[at, :] * kept + total
        mixed = (mixed_in[at, :] * kept + mixed) / total
        for i in range(per):
            out[:, pl.ds((g * per + i) * D, D)] = mixed[i * rows : (i + 1) * rows].astype(
                jnp.bfloat16
            )


VM = pl.BlockSpec(memory_space=pltpu.VMEM)
SM = pl.BlockSpec(memory_space=pltpu.SMEM)
LIMIT = 40 * 1024 * 1024


def local(queries, keys, values, key_norm_gain, stretch_ids, clean_flags, positions):
    rows, width = keys.shape
    heads = queries.shape[1] // D
    groups, per_group = lax.axis_size("stretch"), lax.axis_size("blk")
    blocks = groups * per_group
    tab = jnp.asarray(rope_tables(rows))
    packed = jax.ShapeDtypeStruct((2 * rows + LABEL_ROWS, width), jnp.bfloat16)
    own = pl.pallas_call(
        pack_kernel,
        out_shape=packed,
        in_specs=[SM, SM, SM, VM, VM, VM, VM],
        out_specs=VM,
        compiler_params=pltpu.CompilerParams(vmem_limit_bytes=LIMIT),
        cost_estimate=pl.CostEstimate(flops=10**6, bytes_accessed=4 * 10**5, transcendentals=0),
        name="pack",
    )(stretch_ids, clean_flags, positions, keys, values, key_norm_gain[None, :], tab)

    turned = jax.ShapeDtypeStruct((heads * rows, D), jnp.bfloat16)
    rq, again = pl.pallas_call(
        query_kernel,
        out_shape=(turned, packed),
        in_specs=[SM] + [VM] * 3,
        out_specs=(VM, VM),
        compiler_params=pltpu.CompilerParams(vmem_limit_bytes=LIMIT),
        cost_estimate=pl.CostEstimate(flops=10**6, bytes_accessed=10**6, transcendentals=0),
        name="turn_queries",
    )(positions, queries, own, tab)

    def back(by):
        return lax.ppermute(own, AXES, [(b, b + by) for b in range(blocks - by)])

    def ahead(by):
        pairs = [(b, b - by) for b in range(blocks) if b % per_group >= by]
        return lax.ppermute(again, AXES, pairs)

    b3, b2, b1 = back(3), back(2), back(1)

    def ahead(array, by):
        pairs = [(b, b - by) for b in range(blocks) if b % per_group >= by]
        return lax.ppermute(array, AXES, pairs)

    state = jax.ShapeDtypeStruct((heads * rows, D), jnp.float32)
    def near(own, again, rq):
        a1 = ahead(again, 1)
        a23 = ahead(jnp.concatenate([again, a1], 0), 2)
        done = pl.pallas_call(
            first_kernel,
            out_shape=(state, state, state),
            in_specs=[VM] * 4,
            out_specs=(VM,) * 3,
            compiler_params=pltpu.CompilerParams(vmem_limit_bytes=LIMIT),
            cost_estimate=pl.CostEstimate(
                flops=4 * heads * rows * 4 * rows * D,
                bytes_accessed=3 * 10**6,
                transcendentals=10**6,
            ),
            name="own_and_ahead",
        )(own, a1, a23, rq)
        return tuple(done)

    def never(own, again, rq):
        return (jnp.zeros(state.shape, state.dtype),) * 3

    best, total, mixed = lax.cond(positions[0, 0] >= 0, near, never, own, again, rq)
    return pl.pallas_call(
        last_kernel,
        out_shape=jax.ShapeDtypeStruct((rows, heads * D), jnp.bfloat16),
        in_specs=[VM] * 8,
        out_specs=VM,
        compiler_params=pltpu.CompilerParams(vmem_limit_bytes=LIMIT),
        cost_estimate=pl.CostEstimate(
            flops=4 * heads * rows * 3 * rows * D, bytes_accessed=3 * 10**6, transcendentals=10**6
        ),
        name="back",
    )(own, b1, b2, b3, rq, best, total, mixed)


def solution(mesh):
    placed = (
        P(("stretch", "blk"), "head"),
        P(("stretch", "blk"), "head"),
        P(("stretch", "blk"), "head"),
        P("head"),
        P("stretch", "blk"),
        P("stretch", "blk"),
        P("stretch", "blk"),
    )
    return jax.shard_map(
        local, mesh=mesh, in_specs=placed, out_specs=P(("stretch", "blk"), "head"), check_vma=False
    )
```

```python
import math

import jax
import jax.numpy as jnp
import numpy as np
from jax import lax
from jax.experimental import pallas as pl
from jax.experimental.pallas import tpu as pltpu
from jax.sharding import PartitionSpec as P

D = 128
WINDOW = 3
ROPE_BASE = 10000.0
NEG = -1e30
LABEL_ROWS = 16
AXES = ("stretch", "blk")
SCALE = math.log2(math.e) / math.sqrt(D)


def rope_tables(rows):
    half = D // 2
    f = ROPE_BASE ** (-2.0 * np.arange(half) / D)
    f = np.concatenate([f, f])[None, :]
    t = np.arange(rows, dtype=np.float64)[:, None] * f
    a = 128.0 * np.arange(16, dtype=np.float64)[:, None] * f
    cos = np.concatenate([np.cos(t), np.cos(a)], 0)
    sin = np.concatenate([np.sin(t), np.sin(a)], 0)
    return np.stack([cos, sin]).astype(np.float32)


def angles(pos, tab, rows):
    high = lax.shift_right_logical(pos, 7)
    low = lax.bitwise_and(pos, 127)
    ch, sh = tab[0, pl.ds(rows + high, 1), :], tab[1, pl.ds(rows + high, 1), :]
    cl, sl = tab[0, pl.ds(low, 1), :], tab[1, pl.ds(low, 1), :]
    cp = ch * cl - sh * sl
    sp = sh * cl + ch * sl
    ct, st = tab[0, 0:rows, :], tab[1, 0:rows, :]
    lane = lax.broadcasted_iota(jnp.int32, (1, D), 1)
    sign = jnp.where(lane < D // 2, -1.0, 1.0)
    return cp * ct - sp * st, (sp * ct + cp * st) * sign


def rotate(x, cos, sin):
    return x * cos + pltpu.roll(x, D // 2, 1) * sin


def pack_kernel(
    stretch_hbm, clean_hbm, pos_hbm, k_hbm, v_hbm, gain_hbm, tab_hbm,
    out, turn, stretch, clean, pos, k, gain, tab, sems,
):
    rows = k.shape[0]
    moves = [
        pltpu.make_async_copy(src, dst, sems.at[n])
        for n, (src, dst) in enumerate(
            [
                (k_hbm, k),
                (tab_hbm, tab),
                (pos_hbm, pos),
                (gain_hbm, gain),
                (stretch_hbm, stretch),
                (clean_hbm, clean),
                (v_hbm, out.at[pl.ds(rows, rows)]),
            ]
        )
    ]
    for move in moves:
        move.start()
    for move in moves[:4]:
        move.wait()
    cos, sin = angles(pos[0, 0], tab, rows)
    turn[0] = cos
    turn[1] = sin
    for g in range(k.shape[1] // D):
        cols = pl.ds(g * D, D)
        x = k[:, cols].astype(jnp.float32)
        x = x * lax.rsqrt(jnp.mean(x * x, axis=-1, keepdims=True) + 1e-6) * gain[:, cols]
        out[0:rows, cols] = rotate(x, cos, sin).astype(jnp.bfloat16)
    for move in moves[4:]:
        move.wait()
    label = stretch[0, 0] + 16 * lax.axis_index("stretch")
    row = lax.broadcasted_iota(jnp.int32, (LABEL_ROWS, k.shape[1]), 0)
    info = jnp.where(row == 0, label, jnp.where(row == 1, clean[0, 0], 1))
    out[pl.ds(2 * rows, LABEL_ROWS), :] = info.astype(jnp.float32).astype(jnp.bfloat16)


def labels(ref):
    top = ref.shape[0] - LABEL_ROWS
    info = ref[pl.ds(top, LABEL_ROWS), 0:D].astype(jnp.float32)
    return info[0:1], info[1:2], info[2:3]


def seen(own, other):
    (stretch, clean, _), (stretch2, clean2, there) = own, other
    earlier = (stretch2 < stretch) & (clean2 > 0.5)
    same = (stretch2 == stretch) & (clean2 == clean)
    return (there > 0.5) & (earlier | same)


def scores_of(q, kv, g):
    rows = (kv.shape[0] - LABEL_ROWS) // 2
    keys = kv[0:rows, pl.ds(g * D, D)]
    return lax.dot_general(
        q, keys, (((1,), (1,)), ((), ())), preferred_element_type=jnp.float32
    )


def blend(q, blocks, visible, g, best):
    scores = [scores_of(q, kv, g) for kv in blocks]
    for s, vis in zip(scores, visible):
        top = jnp.where(vis, jnp.max(s, axis=-1, keepdims=True), NEG)
        best = top if best is None else jnp.maximum(best, top)
    shift = best * SCALE
    total, mixed = None, None
    for s, vis, kv in zip(scores, visible, blocks):
        rows = (kv.shape[0] - LABEL_ROWS) // 2
        w = jnp.exp2(s * SCALE - jnp.where(vis, shift, -NEG))
        part = jnp.dot(
            w.astype(jnp.bfloat16),
            kv[pl.ds(rows, rows), pl.ds(g * D, D)],
            preferred_element_type=jnp.float32,
        )
        total = w if total is None else total + w
        mixed = part if mixed is None else mixed + part
    total = jnp.sum(total, axis=-1, keepdims=True)
    return best, total, mixed


def query_kernel(q, own, turn, rq, again):
    rows, heads = q.shape[0], q.shape[1] // D
    cos, sin = turn[0], turn[1]
    again[...] = own[...]
    for h in range(heads):
        x = q[:, pl.ds(h * D, D)].astype(jnp.float32)
        rq[pl.ds(h * rows, rows), :] = rotate(x, cos, sin).astype(jnp.bfloat16)


def first_kernel(own, a1, a2, a3, rq, best_out, total_out, mixed_out):
    rows = (own.shape[0] - LABEL_ROWS) // 2
    groups = own.shape[1] // D
    per = rq.shape[0] // rows // groups
    mine = labels(own)
    blocks = (own, a1, a2, a3)
    visible = [seen(mine, labels(kv)) for kv in blocks]
    for g in range(groups):
        at = pl.ds(g * per * rows, per * rows)
        best, total, mixed = blend(rq[at, :], blocks, visible, g, None)
        best_out[at, :] = jnp.broadcast_to(best, mixed.shape)
        total_out[at, :] = jnp.broadcast_to(total, mixed.shape)
        mixed_out[at, :] = mixed


def last_kernel(b3, b2, b1, own, rq, best_in, total_in, mixed_in, out):
    rows = out.shape[0]
    groups = own.shape[1] // D
    per = rq.shape[0] // rows // groups
    mine = labels(own)
    blocks = (b3, b2, b1)
    visible = [seen(mine, labels(kv)) for kv in blocks]
    for g in range(groups):
        at = pl.ds(g * per * rows, per * rows)
        before = best_in[at, :]
        best, total, mixed = blend(rq[at, :], blocks, visible, g, before)
        kept = jnp.exp2((before - best) * SCALE)
        total = total_in[at, :] * kept + total
        mixed = (mixed_in[at, :] * kept + mixed) / total
        for i in range(per):
            out[:, pl.ds((g * per + i) * D, D)] = mixed[i * rows : (i + 1) * rows].astype(
                jnp.bfloat16
            )


VM = pl.BlockSpec(memory_space=pltpu.VMEM)
HB = pl.BlockSpec(memory_space=pltpu.HBM)
LIMIT = 40 * 1024 * 1024
PACK_LIMIT = 60 * 1024 * 1024
PARAMS = pltpu.CompilerParams(vmem_limit_bytes=LIMIT)


def local(queries, keys, values, key_norm_gain, stretch_ids, clean_flags, positions):
    rows, width = keys.shape
    heads = queries.shape[1] // D
    groups, per_group = lax.axis_size("stretch"), lax.axis_size("blk")
    blocks = groups * per_group
    tab = jnp.asarray(rope_tables(rows))
    packed = jax.ShapeDtypeStruct((2 * rows + LABEL_ROWS, width), jnp.bfloat16)
    own, turn = pl.pallas_call(
        pack_kernel,
        out_shape=(packed, jax.ShapeDtypeStruct((2, rows, D), jnp.float32)),
        in_specs=[HB] * 7,
        out_specs=(VM, VM),
        scratch_shapes=[
            pltpu.SMEM((1, 1), jnp.int32),
            pltpu.SMEM((1, 1), jnp.int32),
            pltpu.SMEM((1, 1), jnp.int32),
            pltpu.VMEM((rows, width), jnp.bfloat16),
            pltpu.VMEM((1, width), jnp.float32),
            pltpu.VMEM(tab.shape, jnp.float32),
            pltpu.SemaphoreType.DMA((7,)),
        ],
        compiler_params=pltpu.CompilerParams(vmem_limit_bytes=PACK_LIMIT),
        cost_estimate=pl.CostEstimate(flops=10**6, bytes_accessed=4 * 10**5, transcendentals=0),
        name="pack",
    )(stretch_ids, clean_flags, positions, keys, values, key_norm_gain[None, :], tab)

    turned = jax.ShapeDtypeStruct((heads * rows, D), jnp.bfloat16)
    rq, again = pl.pallas_call(
        query_kernel,
        out_shape=(turned, packed),
        in_specs=[VM] * 3,
        out_specs=(VM, VM),
        compiler_params=PARAMS,
        cost_estimate=pl.CostEstimate(flops=10**6, bytes_accessed=10**6, transcendentals=0),
        name="turn_queries",
    )(queries, own, turn)

    def back(by):
        return lax.ppermute(own, AXES, [(b, b + by) for b in range(blocks - by)])

    def ahead(array, by):
        pairs = [(b, b - by) for b in range(blocks) if b % per_group >= by]
        return lax.ppermute(array, AXES, pairs)

    b3, b2, b1 = back(3), back(2), back(1)
    state = jax.ShapeDtypeStruct((heads * rows, D), jnp.float32)

    def near(own, again, rq):
        a1, a2 = ahead(again, 1), ahead(again, 2)
        again, a1 = lax.optimization_barrier((again, a1))
        a3 = ahead(again, 3)
        return tuple(
            pl.pallas_call(
                first_kernel,
                out_shape=(state, state, state),
                in_specs=[VM] * 5,
                out_specs=(VM,) * 3,
                compiler_params=PARAMS,
                cost_estimate=pl.CostEstimate(
                    flops=4 * heads * rows * 4 * rows * D,
                    bytes_accessed=3 * 10**6,
                    transcendentals=10**6,
                ),
                name="own_and_ahead",
            )(own, a1, a2, a3, rq)
        )

    def never(own, again, rq):
        return (jnp.zeros(state.shape, state.dtype),) * 3

    best, total, mixed = lax.cond(positions[0, 0] >= 0, near, never, own, again, rq)
    return pl.pallas_call(
        last_kernel,
        out_shape=jax.ShapeDtypeStruct((rows, heads * D), jnp.bfloat16),
        in_specs=[VM] * 8,
        out_specs=VM,
        compiler_params=PARAMS,
        cost_estimate=pl.CostEstimate(
            flops=4 * heads * rows * 3 * rows * D, bytes_accessed=3 * 10**6, transcendentals=10**6
        ),
        name="back",
    )(b3, b2, b1, own, rq, best, total, mixed)


def solution(mesh):
    placed = (
        P(("stretch", "blk"), "head"),
        P(("stretch", "blk"), "head"),
        P(("stretch", "blk"), "head"),
        P("head"),
        P("stretch", "blk"),
        P("stretch", "blk"),
        P("stretch", "blk"),
    )
    return jax.shard_map(
        local, mesh=mesh, in_specs=placed, out_specs=P(("stretch", "blk"), "head"), check_vma=False
    )
```

```python
import math

import jax
import jax.numpy as jnp
import numpy as np
from jax import lax
from jax.experimental import pallas as pl
from jax.experimental.pallas import tpu as pltpu
from jax.sharding import PartitionSpec as P

D = 128
WINDOW = 3
ROW = WINDOW + 1
ROPE_BASE = 10000.0
NEG = -1e30
LABEL_ROWS = 16
AXES = ("stretch", "blk")
SCALE = math.log2(math.e) / math.sqrt(D)


def rope_tables(rows):
    half = D // 2
    f = ROPE_BASE ** (-2.0 * np.arange(half) / D)
    f = np.concatenate([f, f])[None, :]
    t = np.arange(rows, dtype=np.float64)[:, None] * f
    a = 128.0 * np.arange(16, dtype=np.float64)[:, None] * f
    cos = np.concatenate([np.cos(t), np.cos(a)], 0)
    sin = np.concatenate([np.sin(t), np.sin(a)], 0)
    return np.stack([cos, sin]).astype(np.float32)


def angles(pos, tab, rows):
    high = lax.shift_right_logical(pos, 7)
    low = lax.bitwise_and(pos, 127)
    ch, sh = tab[0, pl.ds(rows + high, 1), :], tab[1, pl.ds(rows + high, 1), :]
    cl, sl = tab[0, pl.ds(low, 1), :], tab[1, pl.ds(low, 1), :]
    cp = ch * cl - sh * sl
    sp = sh * cl + ch * sl
    ct, st = tab[0, 0:rows, :], tab[1, 0:rows, :]
    lane = lax.broadcasted_iota(jnp.int32, (1, D), 1)
    sign = jnp.where(lane < D // 2, -1.0, 1.0)
    return cp * ct - sp * st, (sp * ct + cp * st) * sign


def rotate(x, cos, sin):
    return x * cos + pltpu.roll(x, D // 2, 1) * sin


def pack_kernel(
    stretch_hbm, clean_hbm, pos_hbm, k_hbm, v_hbm, gain_hbm, tab_hbm,
    out, turn, stretch, clean, pos, k, gain, tab, sems,
):
    rows = k.shape[0]
    moves = [
        pltpu.make_async_copy(src, dst, sems.at[n])
        for n, (src, dst) in enumerate(
            [
                (k_hbm, k),
                (tab_hbm, tab),
                (pos_hbm, pos),
                (gain_hbm, gain),
                (stretch_hbm, stretch),
                (clean_hbm, clean),
                (v_hbm, out.at[pl.ds(rows, rows)]),
            ]
        )
    ]
    for move in moves:
        move.start()
    for move in moves[:4]:
        move.wait()
    cos, sin = angles(pos[0, 0], tab, rows)
    turn[0] = cos
    turn[1] = sin
    for g in range(k.shape[1] // D):
        cols = pl.ds(g * D, D)
        x = k[:, cols].astype(jnp.float32)
        x = x * lax.rsqrt(jnp.mean(x * x, axis=-1, keepdims=True) + 1e-6) * gain[:, cols]
        out[0:rows, cols] = rotate(x, cos, sin).astype(jnp.bfloat16)
    for move in moves[4:]:
        move.wait()
    label = stretch[0, 0] + 16 * lax.axis_index("stretch")
    row = lax.broadcasted_iota(jnp.int32, (LABEL_ROWS, k.shape[1]), 0)
    info = jnp.where(row == 0, label, jnp.where(row == 1, clean[0, 0], 1))
    out[pl.ds(2 * rows, LABEL_ROWS), :] = info.astype(jnp.float32).astype(jnp.bfloat16)


def labels(ref):
    top = ref.shape[0] - LABEL_ROWS
    info = ref[pl.ds(top, LABEL_ROWS), 0:D].astype(jnp.float32)
    return info[0:1], info[1:2], info[2:3]


def seen(own, other):
    (stretch, clean, _), (stretch2, clean2, there) = own, other
    earlier = (stretch2 < stretch) & (clean2 > 0.5)
    same = (stretch2 == stretch) & (clean2 == clean)
    return (there > 0.5) & (earlier | same)


def scores_of(q, kv, g):
    rows = (kv.shape[0] - LABEL_ROWS) // 2
    keys = kv[0:rows, pl.ds(g * D, D)]
    return lax.dot_general(
        q, keys, (((1,), (1,)), ((), ())), preferred_element_type=jnp.float32
    )


def blend(q, blocks, visible, g, best):
    scores = [scores_of(q, kv, g) for kv in blocks]
    for s, vis in zip(scores, visible):
        top = jnp.where(vis, jnp.max(s, axis=-1, keepdims=True), NEG)
        best = top if best is None else jnp.maximum(best, top)
    shift = best * SCALE
    total, mixed = None, None
    for s, vis, kv in zip(scores, visible, blocks):
        rows = (kv.shape[0] - LABEL_ROWS) // 2
        w = jnp.exp2(s * SCALE - jnp.where(vis, shift, -NEG))
        part = jnp.dot(
            w.astype(jnp.bfloat16),
            kv[pl.ds(rows, rows), pl.ds(g * D, D)],
            preferred_element_type=jnp.float32,
        )
        total = w if total is None else total + w
        mixed = part if mixed is None else mixed + part
    total = jnp.sum(total, axis=-1, keepdims=True)
    return best, total, mixed


def query_kernel(q, own, turn, rq, again):
    rows, heads = q.shape[0], q.shape[1] // D
    cos, sin = turn[0], turn[1]
    again[...] = own[...]
    for h in range(heads):
        x = q[:, pl.ds(h * D, D)].astype(jnp.float32)
        rq[pl.ds(h * rows, rows), :] = rotate(x, cos, sin).astype(jnp.bfloat16)


def first_kernel(own, row, rq, best_out, total_out, mixed_out):
    rows = (own.shape[0] - LABEL_ROWS) // 2
    groups = own.shape[1] // D
    per = rq.shape[0] // rows // groups
    mine = labels(own)
    blocks = [row.at[i] for i in range(ROW)]
    visible = [seen(mine, labels(kv)) for kv in blocks]
    for g in range(groups):
        at = pl.ds(g * per * rows, per * rows)
        best, total, mixed = blend(rq[at, :], blocks, visible, g, None)
        best_out[at, :] = jnp.broadcast_to(best, mixed.shape)
        total_out[at, :] = jnp.broadcast_to(total, mixed.shape)
        mixed_out[at, :] = mixed


def last_kernel(c1, c2, c3, own, rq, best_in, total_in, mixed_in, out):
    rows = out.shape[0]
    groups = own.shape[1] // D
    per = rq.shape[0] // rows // groups
    mine = labels(own)
    blocks = (c1, c2, c3)
    visible = [seen(mine, labels(kv)) for kv in blocks]
    for g in range(groups):
        at = pl.ds(g * per * rows, per * rows)
        before = best_in[at, :]
        best, total, mixed = blend(rq[at, :], blocks, visible, g, before)
        kept = jnp.exp2((before - best) * SCALE)
        total = total_in[at, :] * kept + total
        mixed = (mixed_in[at, :] * kept + mixed) / total
        for i in range(per):
            out[:, pl.ds((g * per + i) * D, D)] = mixed[i * rows : (i + 1) * rows].astype(
                jnp.bfloat16
            )


VM = pl.BlockSpec(memory_space=pltpu.VMEM)
HB = pl.BlockSpec(memory_space=pltpu.HBM)
LIMIT = 40 * 1024 * 1024
PACK_LIMIT = 60 * 1024 * 1024
PARAMS = pltpu.CompilerParams(vmem_limit_bytes=LIMIT)


def local(queries, keys, values, key_norm_gain, stretch_ids, clean_flags, positions):
    rows, width = keys.shape
    heads = queries.shape[1] // D
    groups, per_group = lax.axis_size("stretch"), lax.axis_size("blk")
    blocks = groups * per_group
    tab = jnp.asarray(rope_tables(rows))
    packed = jax.ShapeDtypeStruct((2 * rows + LABEL_ROWS, width), jnp.bfloat16)
    own, turn = pl.pallas_call(
        pack_kernel,
        out_shape=(packed, jax.ShapeDtypeStruct((2, rows, D), jnp.float32)),
        in_specs=[HB] * 7,
        out_specs=(VM, VM),
        scratch_shapes=[
            pltpu.SMEM((1, 1), jnp.int32),
            pltpu.SMEM((1, 1), jnp.int32),
            pltpu.SMEM((1, 1), jnp.int32),
            pltpu.VMEM((rows, width), jnp.bfloat16),
            pltpu.VMEM((1, width), jnp.float32),
            pltpu.VMEM(tab.shape, jnp.float32),
            pltpu.SemaphoreType.DMA((7,)),
        ],
        compiler_params=pltpu.CompilerParams(vmem_limit_bytes=PACK_LIMIT),
        cost_estimate=pl.CostEstimate(flops=10**6, bytes_accessed=4 * 10**5, transcendentals=0),
        name="pack",
    )(stretch_ids, clean_flags, positions, keys, values, key_norm_gain[None, :], tab)

    turned = jax.ShapeDtypeStruct((heads * rows, D), jnp.bfloat16)
    rq, again = pl.pallas_call(
        query_kernel,
        out_shape=(turned, packed),
        in_specs=[VM] * 3,
        out_specs=(VM, VM),
        compiler_params=PARAMS,
        cost_estimate=pl.CostEstimate(flops=10**6, bytes_accessed=10**6, transcendentals=0),
        name="turn_queries",
    )(queries, own, turn)

    def across(by):
        pairs = []
        for b in range(blocks):
            column = (b + by) % ROW
            other = b - b % ROW + column + (-ROW if column > b % ROW else ROW)
            if 0 <= other < blocks and other // per_group <= b // per_group:
                pairs.append((other, b))
        return lax.ppermute(own, AXES, pairs)

    c1, c2, c3 = (across(by) for by in (1, 2, 3))
    line = [list(range(b, b + ROW)) for b in range(0, blocks, ROW)]
    row = lax.all_gather(again, AXES, axis_index_groups=line)
    state = jax.ShapeDtypeStruct((heads * rows, D), jnp.float32)
    best, total, mixed = pl.pallas_call(
        first_kernel,
        out_shape=(state, state, state),
        in_specs=[VM] * 3,
        out_specs=(VM,) * 3,
        compiler_params=PARAMS,
        cost_estimate=pl.CostEstimate(
            flops=4 * heads * rows * 4 * rows * D, bytes_accessed=3 * 10**6, transcendentals=10**6
        ),
        name="row",
    )(own, row, rq)
    return pl.pallas_call(
        last_kernel,
        out_shape=jax.ShapeDtypeStruct((rows, heads * D), jnp.bfloat16),
        in_specs=[VM] * 8,
        out_specs=VM,
        compiler_params=PARAMS,
        cost_estimate=pl.CostEstimate(
            flops=4 * heads * rows * 3 * rows * D, bytes_accessed=3 * 10**6, transcendentals=10**6
        ),
        name="across",
    )(c1, c2, c3, own, rq, best, total, mixed)


def solution(mesh):
    placed = (
        P(("stretch", "blk"), "head"),
        P(("stretch", "blk"), "head"),
        P(("stretch", "blk"), "head"),
        P("head"),
        P("stretch", "blk"),
        P("stretch", "blk"),
        P("stretch", "blk"),
    )
    return jax.shard_map(
        local, mesh=mesh, in_specs=placed, out_specs=P(("stretch", "blk"), "head"), check_vma=False
    )
```

```python
import functools
import math

import jax
import jax.numpy as jnp
import numpy as np
from jax import lax
from jax.experimental import pallas as pl
from jax.experimental.pallas import tpu as pltpu
from jax.sharding import PartitionSpec as P

D = 128
WINDOW = 3
ROW = WINDOW + 1
ROPE_BASE = 10000.0
NEG = -1e30
LABEL_ROWS = 16
AXES = ("stretch", "blk")
SCALE = math.log2(math.e) / math.sqrt(D)


def rope_tables(rows):
    half = D // 2
    f = ROPE_BASE ** (-2.0 * np.arange(half) / D)
    f = np.concatenate([f, f])[None, :]
    t = np.arange(rows, dtype=np.float64)[:, None] * f
    a = 128.0 * np.arange(16, dtype=np.float64)[:, None] * f
    cos = np.concatenate([np.cos(t), np.cos(a)], 0)
    sin = np.concatenate([np.sin(t), np.sin(a)], 0)
    return np.stack([cos, sin]).astype(np.float32)


def angles(pos, tab, rows):
    high = lax.shift_right_logical(pos, 7)
    low = lax.bitwise_and(pos, 127)
    ch, sh = tab[0, pl.ds(rows + high, 1), :], tab[1, pl.ds(rows + high, 1), :]
    cl, sl = tab[0, pl.ds(low, 1), :], tab[1, pl.ds(low, 1), :]
    cp = ch * cl - sh * sl
    sp = sh * cl + ch * sl
    ct, st = tab[0, 0:rows, :], tab[1, 0:rows, :]
    lane = lax.broadcasted_iota(jnp.int32, (1, D), 1)
    sign = jnp.where(lane < D // 2, -1.0, 1.0)
    return cp * ct - sp * st, (sp * ct + cp * st) * sign


def rotate(x, cos, sin):
    return x * cos + pltpu.roll(x, D // 2, 1) * sin


def pack_kernel(
    stretch_hbm, clean_hbm, pos_hbm, k_hbm, v_hbm, gain_hbm, tab_hbm,
    out, stretch, clean, pos, k, gain, tab, sems,
):
    rows = k.shape[0]
    moves = [
        pltpu.make_async_copy(src, dst, sems.at[n])
        for n, (src, dst) in enumerate(
            [
                (k_hbm, k),
                (tab_hbm, tab),
                (pos_hbm, pos),
                (gain_hbm, gain),
                (stretch_hbm, stretch),
                (clean_hbm, clean),
                (v_hbm, out.at[pl.ds(rows, rows)]),
            ]
        )
    ]
    for move in moves:
        move.start()
    for move in moves[:4]:
        move.wait()
    cos, sin = angles(pos[0, 0], tab, rows)
    for g in range(k.shape[1] // D):
        cols = pl.ds(g * D, D)
        x = k[:, cols].astype(jnp.float32)
        x = x * lax.rsqrt(jnp.mean(x * x, axis=-1, keepdims=True) + 1e-6) * gain[:, cols]
        out[0:rows, cols] = rotate(x, cos, sin).astype(jnp.bfloat16)
    for move in moves[4:]:
        move.wait()
    label = stretch[0, 0] + 16 * lax.axis_index("stretch")
    row = lax.broadcasted_iota(jnp.int32, (LABEL_ROWS, k.shape[1]), 0)
    info = jnp.where(row == 0, label, jnp.where(row == 1, clean[0, 0], 1))
    out[pl.ds(2 * rows, LABEL_ROWS), :] = info.astype(jnp.float32).astype(jnp.bfloat16)


def labels(ref):
    top = ref.shape[0] - LABEL_ROWS
    info = ref[pl.ds(top, LABEL_ROWS), 0:D].astype(jnp.float32)
    return info[0:1], info[1:2], info[2:3]


def seen(own, other):
    (stretch, clean, _), (stretch2, clean2, there) = own, other
    earlier = (stretch2 < stretch) & (clean2 > 0.5)
    same = (stretch2 == stretch) & (clean2 == clean)
    return (there > 0.5) & (earlier | same)


def scores_of(q, kv, g):
    rows = (kv.shape[0] - LABEL_ROWS) // 2
    keys = kv[0:rows, pl.ds(g * D, D)]
    return lax.dot_general(
        q, keys, (((1,), (1,)), ((), ())), preferred_element_type=jnp.float32
    )


def blend(q, blocks, visible, g, best):
    scores = [
        jnp.where(vis, scores_of(q, kv, g) * SCALE, NEG) for kv, vis in zip(blocks, visible)
    ]
    top = functools.reduce(jnp.maximum, scores)
    top = jnp.max(top, axis=-1, keepdims=True)
    best = top if best is None else jnp.maximum(best, top)
    total, mixed = None, None
    for s, kv in zip(scores, blocks):
        rows = (kv.shape[0] - LABEL_ROWS) // 2
        w = jnp.exp2(s - best)
        part = jnp.dot(
            w.astype(jnp.bfloat16),
            kv[pl.ds(rows, rows), pl.ds(g * D, D)],
            preferred_element_type=jnp.float32,
        )
        total = w if total is None else total + w
        mixed = part if mixed is None else mixed + part
    return best, jnp.sum(total, axis=-1, keepdims=True), mixed


def first_kernel(pos, own, row, q, tab, rq, best_out, total_out, mixed_out):
    rows = q.shape[0]
    groups = own.shape[1] // D
    per = q.shape[1] // D // groups
    cos, sin = angles(pos[0, 0], tab, rows)
    mine = labels(own)
    blocks = [row.at[i] for i in range(ROW)]
    visible = [seen(mine, labels(kv)) for kv in blocks]
    for g in range(groups):
        at = pl.ds(g * per * rows, per * rows)
        turned = [
            rotate(q[:, pl.ds((g * per + i) * D, D)].astype(jnp.float32), cos, sin)
            for i in range(per)
        ]
        turned = jnp.concatenate([x.astype(jnp.bfloat16) for x in turned], axis=0)
        rq[at, :] = turned
        best, total, mixed = blend(turned, blocks, visible, g, None)
        best_out[at, :] = jnp.broadcast_to(best, mixed.shape)
        total_out[at, :] = jnp.broadcast_to(total, mixed.shape)
        mixed_out[at, :] = mixed


def last_kernel(c1, c2, c3, own, rq, best_in, total_in, mixed_in, out):
    rows = out.shape[0]
    groups = own.shape[1] // D
    per = rq.shape[0] // rows // groups
    mine = labels(own)
    blocks = (c1, c2, c3)
    visible = [seen(mine, labels(kv)) for kv in blocks]
    for g in range(groups):
        at = pl.ds(g * per * rows, per * rows)
        before = best_in[at, :]
        best, total, mixed = blend(rq[at, :], blocks, visible, g, before)
        kept = jnp.exp2(before - best)
        total = total_in[at, :] * kept + total
        mixed = (mixed_in[at, :] * kept + mixed) / total
        for i in range(per):
            out[:, pl.ds((g * per + i) * D, D)] = mixed[i * rows : (i + 1) * rows].astype(
                jnp.bfloat16
            )


VM = pl.BlockSpec(memory_space=pltpu.VMEM)
SM = pl.BlockSpec(memory_space=pltpu.SMEM)
HB = pl.BlockSpec(memory_space=pltpu.HBM)
LIMIT = 40 * 1024 * 1024
PACK_LIMIT = 60 * 1024 * 1024
PARAMS = pltpu.CompilerParams(vmem_limit_bytes=LIMIT)


def local(queries, keys, values, key_norm_gain, stretch_ids, clean_flags, positions):
    rows, width = keys.shape
    heads = queries.shape[1] // D
    groups, per_group = lax.axis_size("stretch"), lax.axis_size("blk")
    blocks = groups * per_group
    tab = jnp.asarray(rope_tables(rows))
    packed = jax.ShapeDtypeStruct((2 * rows + LABEL_ROWS, width), jnp.bfloat16)
    own = pl.pallas_call(
        pack_kernel,
        out_shape=packed,
        in_specs=[HB] * 7,
        out_specs=VM,
        scratch_shapes=[
            pltpu.SMEM((1, 1), jnp.int32),
            pltpu.SMEM((1, 1), jnp.int32),
            pltpu.SMEM((1, 1), jnp.int32),
            pltpu.VMEM((rows, width), jnp.bfloat16),
            pltpu.VMEM((1, width), jnp.float32),
            pltpu.VMEM(tab.shape, jnp.float32),
            pltpu.SemaphoreType.DMA((7,)),
        ],
        compiler_params=pltpu.CompilerParams(vmem_limit_bytes=PACK_LIMIT),
        cost_estimate=pl.CostEstimate(flops=10**6, bytes_accessed=4 * 10**5, transcendentals=0),
        name="pack",
    )(stretch_ids, clean_flags, positions, keys, values, key_norm_gain[None, :], tab)

    def across(by):
        pairs = []
        for b in range(blocks):
            column = (b + by) % ROW
            other = b - b % ROW + column + (-ROW if column > b % ROW else ROW)
            if 0 <= other < blocks and other // per_group <= b // per_group:
                pairs.append((other, b))
        return lax.ppermute(own, AXES, pairs)

    c1, c2, c3 = (across(by) for by in (1, 2, 3))
    line = [list(range(b, b + ROW)) for b in range(0, blocks, ROW)]
    row = lax.all_gather(own, AXES, axis_index_groups=line)
    state = jax.ShapeDtypeStruct((heads * rows, D), jnp.float32)
    rq, best, total, mixed = pl.pallas_call(
        first_kernel,
        out_shape=(jax.ShapeDtypeStruct((heads * rows, D), jnp.bfloat16), state, state, state),
        in_specs=[SM] + [VM] * 4,
        out_specs=(VM,) * 4,
        compiler_params=PARAMS,
        cost_estimate=pl.CostEstimate(
            flops=4 * heads * rows * 4 * rows * D, bytes_accessed=3 * 10**6, transcendentals=10**6
        ),
        name="row",
    )(positions, own, row, queries, tab)
    return pl.pallas_call(
        last_kernel,
        out_shape=jax.ShapeDtypeStruct((rows, heads * D), jnp.bfloat16),
        in_specs=[VM] * 8,
        out_specs=VM,
        compiler_params=PARAMS,
        cost_estimate=pl.CostEstimate(
            flops=4 * heads * rows * 3 * rows * D, bytes_accessed=3 * 10**6, transcendentals=10**6
        ),
        name="across",
    )(c1, c2, c3, own, rq, best, total, mixed)


def solution(mesh):
    placed = (
        P(("stretch", "blk"), "head"),
        P(("stretch", "blk"), "head"),
        P(("stretch", "blk"), "head"),
        P("head"),
        P("stretch", "blk"),
        P("stretch", "blk"),
        P("stretch", "blk"),
    )
    return jax.shard_map(
        local, mesh=mesh, in_specs=placed, out_specs=P(("stretch", "blk"), "head"), check_vma=False
    )
```

```python
import functools
import math

import jax
import jax.numpy as jnp
import numpy as np
from jax import lax
from jax.experimental import pallas as pl
from jax.experimental.pallas import tpu as pltpu
from jax.sharding import PartitionSpec as P

D = 128
WINDOW = 3
ROW = WINDOW + 1
CHUNK = 2
ROPE_BASE = 10000.0
NEG = -1e30
LABEL_ROWS = 8
AXES = ("stretch", "blk")
SCALE = math.log2(math.e) / math.sqrt(D)


def rope_tables(rows):
    half = D // 2
    f = ROPE_BASE ** (-2.0 * np.arange(half) / D)
    f = np.concatenate([f, f])[None, :]
    t = np.arange(rows, dtype=np.float64)[:, None] * f
    a = 128.0 * np.arange(16, dtype=np.float64)[:, None] * f
    cos = np.concatenate([np.cos(t), np.cos(a)], 0)
    sin = np.concatenate([np.sin(t), np.sin(a)], 0)
    return np.stack([cos, sin]).astype(np.float32)


def angles(pos, tab, rows):
    high = lax.shift_right_logical(pos, 7)
    low = lax.bitwise_and(pos, 127)
    ch, sh = tab[0, pl.ds(rows + high, 1), :], tab[1, pl.ds(rows + high, 1), :]
    cl, sl = tab[0, pl.ds(low, 1), :], tab[1, pl.ds(low, 1), :]
    cp = ch * cl - sh * sl
    sp = sh * cl + ch * sl
    ct, st = tab[0, 0:rows, :], tab[1, 0:rows, :]
    lane = lax.broadcasted_iota(jnp.int32, (1, D), 1)
    sign = jnp.where(lane < D // 2, -1.0, 1.0)
    return cp * ct - sp * st, (sp * ct + cp * st) * sign


def rotate(x, cos, sin):
    return x * cos + pltpu.roll(x, D // 2, 1) * sin


def pack_kernel(
    stretch, clean, pos, k_hbm, v_hbm, gain_hbm, tab_hbm,
    out, k, gain, tab, sems,
):
    rows = k.shape[0]
    moves = [
        pltpu.make_async_copy(src, dst, sems.at[n])
        for n, (src, dst) in enumerate(
            [
                (k_hbm, k),
                (tab_hbm, tab),
                (gain_hbm, gain),
                (v_hbm, out.at[pl.ds(rows, rows)]),
            ]
        )
    ]
    for move in moves:
        move.start()
    for move in moves[:3]:
        move.wait()
    cos, sin = angles(pos[0, 0], tab, rows)
    for g in range(k.shape[1] // D):
        cols = pl.ds(g * D, D)
        x = k[:, cols].astype(jnp.float32)
        x = x * lax.rsqrt(jnp.mean(x * x, axis=-1, keepdims=True) + 1e-6) * gain[:, cols]
        out[0:rows, cols] = rotate(x, cos, sin).astype(jnp.bfloat16)
    for move in moves[3:]:
        move.wait()
    label = stretch[0, 0] + 16 * lax.axis_index("stretch")
    row = lax.broadcasted_iota(jnp.int32, (LABEL_ROWS, k.shape[1]), 0)
    info = jnp.where(row == 0, label, jnp.where(row == 1, clean[0, 0], 1))
    out[pl.ds(2 * rows, LABEL_ROWS), :] = info.astype(jnp.float32).astype(jnp.bfloat16)


def labels(ref):
    top = ref.shape[0] - LABEL_ROWS
    info = ref[pl.ds(top, LABEL_ROWS), 0:D].astype(jnp.float32)
    return info[0:1], info[1:2], info[2:3]


def seen(own, other):
    (stretch, clean, _), (stretch2, clean2, there) = own, other
    earlier = (stretch2 < stretch) & (clean2 > 0.5)
    same = (stretch2 == stretch) & (clean2 == clean)
    return (there > 0.5) & (earlier | same)


def cross(a, b, over_a, over_b):
    return lax.dot_general(
        a, b, (((over_a,), (over_b,)), ((), ())), preferred_element_type=jnp.float32
    )


def blend(q, blocks, bias, g, best):
    cols = pl.ds(g * D, D)
    scores = []
    for kv, hidden in zip(blocks, bias):
        rows = (kv.shape[0] - LABEL_ROWS) // 2
        scores.append(cross(kv[0:rows, cols], q, 1, 1) * SCALE + hidden)
    top = functools.reduce(jnp.maximum, scores)
    top = jnp.max(top, axis=0, keepdims=True)
    best = top if best is None else jnp.maximum(best, top)
    total, mixed = None, None
    for s, kv in zip(scores, blocks):
        rows = (kv.shape[0] - LABEL_ROWS) // 2
        w = jnp.exp2(s - best)
        part = cross(kv[pl.ds(rows, rows), cols], w.astype(jnp.bfloat16), 0, 0)
        total = w if total is None else total + w
        mixed = part if mixed is None else mixed + part
    return best, jnp.sum(total, axis=0, keepdims=True), mixed


def hidden_by(mine, blocks):
    bias = [jnp.where(seen(mine, labels(kv)), 0.0, NEG) for kv in blocks]
    return [jnp.concatenate([b] * CHUNK, axis=1) for b in bias]


def first_kernel(pos, own, row, q, tab, rq, stat_out, mixed_out):
    rows = q.shape[0]
    groups = own.shape[1] // D
    per = q.shape[1] // D // groups
    cos, sin = angles(pos[0, 0], tab, rows)
    blocks = [row.at[i] for i in range(ROW)]
    bias = hidden_by(labels(own), blocks)
    for head in range(0, groups * per, CHUNK):
        turned = [
            rotate(q[:, pl.ds((head + i) * D, D)].astype(jnp.float32), cos, sin)
            for i in range(CHUNK)
        ]
        turned = jnp.concatenate([x.astype(jnp.bfloat16) for x in turned], axis=0)
        rq[pl.ds(head * rows, CHUNK * rows), :] = turned
        best, total, mixed = blend(turned, blocks, bias, head // per, None)
        cols = pl.ds(head * rows, CHUNK * rows)
        stat_out[0:1, cols] = best
        stat_out[1:2, cols] = total
        mixed_out[:, cols] = mixed


def last_kernel(c1, c2, c3, own, rq, stat, mixed_in, out_hbm, out, sems):
    rows = out.shape[0]
    groups = own.shape[1] // D
    per = rq.shape[0] // rows // groups
    blocks = (c1, c2, c3)
    bias = hidden_by(labels(own), blocks)
    moves = []
    for head in range(0, groups * per, CHUNK):
        at = pl.ds(head * rows, CHUNK * rows)
        before = stat[0:1, at]
        best, total, mixed = blend(rq[at, :], blocks, bias, head // per, before)
        kept = jnp.exp2(before - best)
        share = 1.0 / (stat[1:2, at] * kept + total)
        mixed = mixed_in[:, at] * (kept * share) + mixed * share
        for i in range(CHUNK):
            one = mixed[:, i * rows : (i + 1) * rows]
            out[:, pl.ds((head + i) * D, D)] = one.T.astype(jnp.bfloat16)
        cols = pl.ds(head * D, CHUNK * D)
        moves.append(
            pltpu.make_async_copy(out.at[:, cols], out_hbm.at[:, cols], sems.at[head // CHUNK])
        )
        moves[-1].start()
    for move in moves:
        move.wait()


VM = pl.BlockSpec(memory_space=pltpu.VMEM)
SM = pl.BlockSpec(memory_space=pltpu.SMEM)
HB = pl.BlockSpec(memory_space=pltpu.HBM)
LIMIT = 40 * 1024 * 1024
PACK_LIMIT = 60 * 1024 * 1024
PARAMS = pltpu.CompilerParams(vmem_limit_bytes=LIMIT)


def local(queries, keys, values, key_norm_gain, stretch_ids, clean_flags, positions):
    rows, width = keys.shape
    heads = queries.shape[1] // D
    groups, per_group = lax.axis_size("stretch"), lax.axis_size("blk")
    blocks = groups * per_group
    tab = jnp.asarray(rope_tables(rows))
    packed = jax.ShapeDtypeStruct((2 * rows + LABEL_ROWS, width), jnp.bfloat16)
    own = pl.pallas_call(
        pack_kernel,
        out_shape=packed,
        in_specs=[SM] * 3 + [HB] * 4,
        out_specs=VM,
        scratch_shapes=[
            pltpu.VMEM((rows, width), jnp.bfloat16),
            pltpu.VMEM((1, width), jnp.float32),
            pltpu.VMEM(tab.shape, jnp.float32),
            pltpu.SemaphoreType.DMA((4,)),
        ],
        compiler_params=pltpu.CompilerParams(vmem_limit_bytes=PACK_LIMIT),
        cost_estimate=pl.CostEstimate(flops=10**6, bytes_accessed=4 * 10**5, transcendentals=0),
        name="pack",
    )(stretch_ids, clean_flags, positions, keys, values, key_norm_gain[None, :], tab)

    def across(by):
        pairs = []
        for b in range(blocks):
            column = (b + by) % ROW
            other = b - b % ROW + column + (-ROW if column > b % ROW else ROW)
            if 0 <= other < blocks and other // per_group <= b // per_group:
                pairs.append((other, b))
        return lax.ppermute(own, AXES, pairs)

    c1, c2, c3 = (across(by) for by in (1, 2, 3))
    line = [list(range(b, b + ROW)) for b in range(0, blocks, ROW)]
    row = lax.all_gather(own, AXES, axis_index_groups=line)
    rq, stat, mixed = pl.pallas_call(
        first_kernel,
        out_shape=(
            jax.ShapeDtypeStruct((heads * rows, D), jnp.bfloat16),
            jax.ShapeDtypeStruct((8, heads * rows), jnp.float32),
            jax.ShapeDtypeStruct((D, heads * rows), jnp.float32),
        ),
        in_specs=[SM] + [VM] * 4,
        out_specs=(VM,) * 3,
        compiler_params=PARAMS,
        cost_estimate=pl.CostEstimate(
            flops=4 * heads * rows * 4 * rows * D, bytes_accessed=3 * 10**6, transcendentals=10**6
        ),
        name="row",
    )(positions, own, row, queries, tab)
    return pl.pallas_call(
        last_kernel,
        out_shape=jax.ShapeDtypeStruct((rows, heads * D), jnp.bfloat16),
        in_specs=[VM] * 7,
        out_specs=HB,
        scratch_shapes=[
            pltpu.VMEM((rows, heads * D), jnp.bfloat16),
            pltpu.SemaphoreType.DMA((heads // CHUNK,)),
        ],
        compiler_params=PARAMS,
        cost_estimate=pl.CostEstimate(
            flops=4 * heads * rows * 3 * rows * D, bytes_accessed=3 * 10**6, transcendentals=10**6
        ),
        name="across",
    )(c1, c2, c3, own, rq, stat, mixed)


def solution(mesh):
    placed = (
        P(("stretch", "blk"), "head"),
        P(("stretch", "blk"), "head"),
        P(("stretch", "blk"), "head"),
        P("head"),
        P("stretch", "blk"),
        P("stretch", "blk"),
        P("stretch", "blk"),
    )
    return jax.shard_map(
        local, mesh=mesh, in_specs=placed, out_specs=P(("stretch", "blk"), "head"), check_vma=False
    )
```

```python
import functools
import math

import jax
import jax.numpy as jnp
import numpy as np
from jax import lax
from jax.experimental import pallas as pl
from jax.experimental.pallas import tpu as pltpu
from jax.sharding import PartitionSpec as P

D = 128
WINDOW = 3
ROW = WINDOW + 1
CHUNK = 2
ROPE_BASE = 10000.0
NEG = -1e30
LABEL_ROWS = 8
AXES = ("stretch", "blk")
SCALE = math.log2(math.e) / math.sqrt(D)


def rope_tables(rows):
    half = D // 2
    f = ROPE_BASE ** (-2.0 * np.arange(half) / D)
    f = np.concatenate([f, f])[None, :]
    t = np.arange(rows, dtype=np.float64)[:, None] * f
    a = 128.0 * np.arange(16, dtype=np.float64)[:, None] * f
    cos = np.concatenate([np.cos(t), np.cos(a)], 0)
    sin = np.concatenate([np.sin(t), np.sin(a)], 0)
    return np.stack([cos, sin]).astype(np.float32)


def angles(pos, tab, rows):
    high = lax.shift_right_logical(pos, 7)
    low = lax.bitwise_and(pos, 127)
    ch, sh = tab[0, pl.ds(rows + high, 1), :], tab[1, pl.ds(rows + high, 1), :]
    cl, sl = tab[0, pl.ds(low, 1), :], tab[1, pl.ds(low, 1), :]
    cp = ch * cl - sh * sl
    sp = sh * cl + ch * sl
    ct, st = tab[0, 0:rows, :], tab[1, 0:rows, :]
    lane = lax.broadcasted_iota(jnp.int32, (1, D), 1)
    sign = jnp.where(lane < D // 2, -1.0, 1.0)
    return cp * ct - sp * st, (sp * ct + cp * st) * sign


def rotate(x, cos, sin):
    return x * cos + pltpu.roll(x, D // 2, 1) * sin


def pack_kernel(
    stretch, clean, pos, k_hbm, v_hbm, gain_hbm, tab_hbm,
    out, k, gain, tab, sems,
):
    rows = k.shape[0]
    moves = [
        pltpu.make_async_copy(src, dst, sems.at[n])
        for n, (src, dst) in enumerate(
            [
                (k_hbm, k),
                (tab_hbm, tab),
                (gain_hbm, gain),
                (v_hbm, out.at[pl.ds(rows, rows)]),
            ]
        )
    ]
    for move in moves:
        move.start()
    for move in moves[:3]:
        move.wait()
    cos, sin = angles(pos[0, 0], tab, rows)
    for g in range(k.shape[1] // D):
        cols = pl.ds(g * D, D)
        x = k[:, cols].astype(jnp.float32)
        x = x * lax.rsqrt(jnp.mean(x * x, axis=-1, keepdims=True) + 1e-6) * gain[:, cols]
        out[0:rows, cols] = rotate(x, cos, sin).astype(jnp.bfloat16)
    for move in moves[3:]:
        move.wait()
    label = stretch[0, 0] + 16 * lax.axis_index("stretch")
    row = lax.broadcasted_iota(jnp.int32, (LABEL_ROWS, k.shape[1]), 0)
    info = jnp.where(row == 0, label, jnp.where(row == 1, clean[0, 0], 1))
    out[pl.ds(2 * rows, LABEL_ROWS), :] = info.astype(jnp.float32).astype(jnp.bfloat16)


def labels(ref):
    top = ref.shape[0] - LABEL_ROWS
    info = ref[pl.ds(top, LABEL_ROWS), 0:D].astype(jnp.float32)
    return info[0:1], info[1:2], info[2:3]


def seen(own, other):
    (stretch, clean, _), (stretch2, clean2, there) = own, other
    earlier = (stretch2 < stretch) & (clean2 > 0.5)
    same = (stretch2 == stretch) & (clean2 == clean)
    return (there > 0.5) & (earlier | same)


def cross(a, b, over_a, over_b):
    return lax.dot_general(
        a, b, (((over_a,), (over_b,)), ((), ())), preferred_element_type=jnp.float32
    )


def blend(q, blocks, bias, g, best):
    cols = pl.ds(g * D, D)
    scores = []
    for kv, hidden in zip(blocks, bias):
        rows = (kv.shape[0] - LABEL_ROWS) // 2
        scores.append(cross(kv[0:rows, cols], q, 1, 1) * SCALE + hidden)
    top = functools.reduce(jnp.maximum, scores)
    top = jnp.max(top, axis=0, keepdims=True)
    best = top if best is None else jnp.maximum(best, top)
    total, mixed = None, None
    for s, kv in zip(scores, blocks):
        rows = (kv.shape[0] - LABEL_ROWS) // 2
        w = jnp.exp2(s - best)
        part = cross(kv[pl.ds(rows, rows), cols], w.astype(jnp.bfloat16), 0, 0)
        total = w if total is None else total + w
        mixed = part if mixed is None else mixed + part
    return best, jnp.sum(total, axis=0, keepdims=True), mixed


def hidden_by(mine, blocks):
    bias = [jnp.where(seen(mine, labels(kv)), 0.0, NEG) for kv in blocks]
    return [jnp.concatenate([b] * CHUNK, axis=1) for b in bias]


def first_kernel(pos, own, row, q, tab, rq, stat_out, mixed_out):
    rows = q.shape[0]
    groups = own.shape[1] // D
    per = q.shape[1] // D // groups
    cos, sin = angles(pos[0, 0], tab, rows)
    blocks = [row.at[i] for i in range(ROW)]
    bias = hidden_by(labels(own), blocks)
    for head in range(0, groups * per, CHUNK):
        turned = [
            rotate(q[:, pl.ds((head + i) * D, D)].astype(jnp.float32), cos, sin)
            for i in range(CHUNK)
        ]
        turned = jnp.concatenate([x.astype(jnp.bfloat16) for x in turned], axis=0)
        rq[pl.ds(head * rows, CHUNK * rows), :] = turned
        best, total, mixed = blend(turned, blocks, bias, head // per, None)
        cols = pl.ds(head * rows, CHUNK * rows)
        stat_out[0:1, cols] = best
        stat_out[1:2, cols] = total
        mixed_out[:, cols] = mixed


def last_kernel(c2, c3, c1, own, rq, stat, mixed_in, out_hbm, out, sems):
    rows = out.shape[0]
    groups = own.shape[1] // D
    per = rq.shape[0] // rows // groups
    blocks = (c2, c3, c1)
    bias = hidden_by(labels(own), blocks)
    moves = []
    for head in range(0, groups * per, CHUNK):
        at = pl.ds(head * rows, CHUNK * rows)
        before = stat[0:1, at]
        best, total, mixed = blend(rq[at, :], blocks, bias, head // per, before)
        kept = jnp.exp2(before - best)
        share = 1.0 / (stat[1:2, at] * kept + total)
        mixed = mixed_in[:, at] * (kept * share) + mixed * share
        for i in range(CHUNK):
            one = mixed[:, i * rows : (i + 1) * rows]
            out[:, pl.ds((head + i) * D, D)] = one.T.astype(jnp.bfloat16)
        cols = pl.ds(head * D, CHUNK * D)
        moves.append(
            pltpu.make_async_copy(out.at[:, cols], out_hbm.at[:, cols], sems.at[head // CHUNK])
        )
        moves[-1].start()
    for move in moves:
        move.wait()


VM = pl.BlockSpec(memory_space=pltpu.VMEM)
SM = pl.BlockSpec(memory_space=pltpu.SMEM)
HB = pl.BlockSpec(memory_space=pltpu.HBM)
LIMIT = 40 * 1024 * 1024
PACK_LIMIT = 60 * 1024 * 1024
PARAMS = pltpu.CompilerParams(vmem_limit_bytes=LIMIT)


def local(queries, keys, values, key_norm_gain, stretch_ids, clean_flags, positions):
    rows, width = keys.shape
    heads = queries.shape[1] // D
    groups, per_group = lax.axis_size("stretch"), lax.axis_size("blk")
    blocks = groups * per_group
    tab = jnp.asarray(rope_tables(rows))
    packed = jax.ShapeDtypeStruct((2 * rows + LABEL_ROWS, width), jnp.bfloat16)
    own = pl.pallas_call(
        pack_kernel,
        out_shape=packed,
        in_specs=[SM] * 3 + [HB] * 4,
        out_specs=VM,
        scratch_shapes=[
            pltpu.VMEM((rows, width), jnp.bfloat16),
            pltpu.VMEM((1, width), jnp.float32),
            pltpu.VMEM(tab.shape, jnp.float32),
            pltpu.SemaphoreType.DMA((4,)),
        ],
        compiler_params=pltpu.CompilerParams(vmem_limit_bytes=PACK_LIMIT),
        cost_estimate=pl.CostEstimate(flops=10**6, bytes_accessed=4 * 10**5, transcendentals=0),
        name="pack",
    )(stretch_ids, clean_flags, positions, keys, values, key_norm_gain[None, :], tab)

    def across(by):
        pairs = []
        for b in range(blocks):
            column = (b + by) % ROW
            other = b - b % ROW + column + (-ROW if column > b % ROW else ROW)
            if 0 <= other < blocks and other // per_group <= b // per_group:
                pairs.append((other, b))
        return lax.ppermute(own, AXES, pairs)

    c1, c2, c3 = (across(by) for by in (1, 2, 3))
    line = [list(range(b, b + ROW)) for b in range(0, blocks, ROW)]
    row = lax.all_gather(own, AXES, axis_index_groups=line)
    rq, stat, mixed = pl.pallas_call(
        first_kernel,
        out_shape=(
            jax.ShapeDtypeStruct((heads * rows, D), jnp.bfloat16),
            jax.ShapeDtypeStruct((8, heads * rows), jnp.float32),
            jax.ShapeDtypeStruct((D, heads * rows), jnp.float32),
        ),
        in_specs=[SM] + [VM] * 4,
        out_specs=(VM,) * 3,
        compiler_params=PARAMS,
        cost_estimate=pl.CostEstimate(
            flops=4 * heads * rows * 4 * rows * D, bytes_accessed=3 * 10**6, transcendentals=10**6
        ),
        name="row",
    )(positions, own, row, queries, tab)
    return pl.pallas_call(
        last_kernel,
        out_shape=jax.ShapeDtypeStruct((rows, heads * D), jnp.bfloat16),
        in_specs=[VM] * 7,
        out_specs=HB,
        scratch_shapes=[
            pltpu.VMEM((rows, heads * D), jnp.bfloat16),
            pltpu.SemaphoreType.DMA((heads // CHUNK,)),
        ],
        compiler_params=PARAMS,
        cost_estimate=pl.CostEstimate(
            flops=4 * heads * rows * 3 * rows * D, bytes_accessed=3 * 10**6, transcendentals=10**6
        ),
        name="across",
    )(c2, c3, c1, own, rq, stat, mixed)


def solution(mesh):
    placed = (
        P(("stretch", "blk"), "head"),
        P(("stretch", "blk"), "head"),
        P(("stretch", "blk"), "head"),
        P("head"),
        P("stretch", "blk"),
        P("stretch", "blk"),
        P("stretch", "blk"),
    )
    return jax.shard_map(
        local, mesh=mesh, in_specs=placed, out_specs=P(("stretch", "blk"), "head"), check_vma=False
    )
```

```python
import functools
import math

import jax
import jax.numpy as jnp
import numpy as np
from jax import lax
from jax.experimental import pallas as pl
from jax.experimental.pallas import tpu as pltpu
from jax.sharding import PartitionSpec as P

D = 128
WINDOW = 3
ROW = WINDOW + 1
SOURCES = ((2, 0, 3, 1), (1, 3, 0, 2), (3, 2, 1, 0))
CHUNK = 2
ROPE_BASE = 10000.0
NEG = -1e30
LABEL_ROWS = 8
AXES = ("stretch", "blk")
SCALE = math.log2(math.e) / math.sqrt(D)


def rope_tables(rows):
    half = D // 2
    f = ROPE_BASE ** (-2.0 * np.arange(half) / D)
    f = np.concatenate([f, f])[None, :]
    t = np.arange(rows, dtype=np.float64)[:, None] * f
    a = 128.0 * np.arange(16, dtype=np.float64)[:, None] * f
    cos = np.concatenate([np.cos(t), np.cos(a)], 0)
    sin = np.concatenate([np.sin(t), np.sin(a)], 0)
    return np.stack([cos, sin]).astype(np.float32)


def angles(pos, tab, rows):
    high = lax.shift_right_logical(pos, 7)
    low = lax.bitwise_and(pos, 127)
    ch, sh = tab[0, pl.ds(rows + high, 1), :], tab[1, pl.ds(rows + high, 1), :]
    cl, sl = tab[0, pl.ds(low, 1), :], tab[1, pl.ds(low, 1), :]
    cp = ch * cl - sh * sl
    sp = sh * cl + ch * sl
    ct, st = tab[0, 0:rows, :], tab[1, 0:rows, :]
    lane = lax.broadcasted_iota(jnp.int32, (1, D), 1)
    sign = jnp.where(lane < D // 2, -1.0, 1.0)
    return cp * ct - sp * st, (sp * ct + cp * st) * sign


def rotate(x, cos, sin):
    return x * cos + pltpu.roll(x, D // 2, 1) * sin


def pack_kernel(
    stretch, clean, pos, k_hbm, v_hbm, gain_hbm, tab_hbm,
    out, k, gain, tab, sems,
):
    rows = k.shape[0]
    moves = [
        pltpu.make_async_copy(src, dst, sems.at[n])
        for n, (src, dst) in enumerate(
            [
                (k_hbm, k),
                (tab_hbm, tab),
                (gain_hbm, gain),
                (v_hbm, out.at[pl.ds(rows, rows)]),
            ]
        )
    ]
    for move in moves:
        move.start()
    for move in moves[:3]:
        move.wait()
    cos, sin = angles(pos[0, 0], tab, rows)
    for g in range(k.shape[1] // D):
        cols = pl.ds(g * D, D)
        x = k[:, cols].astype(jnp.float32)
        x = x * lax.rsqrt(jnp.mean(x * x, axis=-1, keepdims=True) + 1e-6) * gain[:, cols]
        out[0:rows, cols] = rotate(x, cos, sin).astype(jnp.bfloat16)
    for move in moves[3:]:
        move.wait()
    label = stretch[0, 0] + 16 * lax.axis_index("stretch")
    row = lax.broadcasted_iota(jnp.int32, (LABEL_ROWS, k.shape[1]), 0)
    info = jnp.where(row == 0, label, jnp.where(row == 1, clean[0, 0], 1))
    out[pl.ds(2 * rows, LABEL_ROWS), :] = info.astype(jnp.float32).astype(jnp.bfloat16)


def labels(ref):
    top = ref.shape[0] - LABEL_ROWS
    info = ref[pl.ds(top, LABEL_ROWS), 0:D].astype(jnp.float32)
    return info[0:1], info[1:2], info[2:3]


def seen(own, other):
    (stretch, clean, _), (stretch2, clean2, there) = own, other
    earlier = (stretch2 < stretch) & (clean2 > 0.5)
    same = (stretch2 == stretch) & (clean2 == clean)
    return (there > 0.5) & (earlier | same)


def cross(a, b, over_a, over_b):
    return lax.dot_general(
        a, b, (((over_a,), (over_b,)), ((), ())), preferred_element_type=jnp.float32
    )


def blend(q, blocks, bias, g, best):
    cols = pl.ds(g * D, D)
    scores = []
    for kv, hidden in zip(blocks, bias):
        rows = (kv.shape[0] - LABEL_ROWS) // 2
        scores.append(cross(kv[0:rows, cols], q, 1, 1) * SCALE + hidden)
    top = functools.reduce(jnp.maximum, scores)
    top = jnp.max(top, axis=0, keepdims=True)
    best = top if best is None else jnp.maximum(best, top)
    total, mixed = None, None
    for s, kv in zip(scores, blocks):
        rows = (kv.shape[0] - LABEL_ROWS) // 2
        w = jnp.exp2(s - best)
        part = cross(kv[pl.ds(rows, rows), cols], w.astype(jnp.bfloat16), 0, 0)
        total = w if total is None else total + w
        mixed = part if mixed is None else mixed + part
    return best, jnp.sum(total, axis=0, keepdims=True), mixed


def hidden_by(mine, blocks):
    bias = [jnp.where(seen(mine, labels(kv)), 0.0, NEG) for kv in blocks]
    return [jnp.concatenate([b] * CHUNK, axis=1) for b in bias]


def first_kernel(pos, own, row, q, tab, rq, stat_out, mixed_out):
    rows = q.shape[0]
    groups = own.shape[1] // D
    per = q.shape[1] // D // groups
    cos, sin = angles(pos[0, 0], tab, rows)
    blocks = [row.at[i] for i in range(ROW)]
    bias = hidden_by(labels(own), blocks)
    for head in range(0, groups * per, CHUNK):
        turned = [
            rotate(q[:, pl.ds((head + i) * D, D)].astype(jnp.float32), cos, sin)
            for i in range(CHUNK)
        ]
        turned = jnp.concatenate([x.astype(jnp.bfloat16) for x in turned], axis=0)
        rq[pl.ds(head * rows, CHUNK * rows), :] = turned
        best, total, mixed = blend(turned, blocks, bias, head // per, None)
        cols = pl.ds(head * rows, CHUNK * rows)
        stat_out[0:1, cols] = best
        stat_out[1:2, cols] = total
        mixed_out[:, cols] = mixed


def last_kernel(c1, c2, c3, own, rq, stat, mixed_in, out_hbm, out, sems):
    rows = out.shape[0]
    groups = own.shape[1] // D
    per = rq.shape[0] // rows // groups
    blocks = (c1, c2, c3)
    bias = hidden_by(labels(own), blocks)
    moves = []
    for head in range(0, groups * per, CHUNK):
        at = pl.ds(head * rows, CHUNK * rows)
        before = stat[0:1, at]
        best, total, mixed = blend(rq[at, :], blocks, bias, head // per, before)
        kept = jnp.exp2(before - best)
        share = 1.0 / (stat[1:2, at] * kept + total)
        mixed = mixed_in[:, at] * (kept * share) + mixed * share
        for i in range(CHUNK):
            one = mixed[:, i * rows : (i + 1) * rows]
            out[:, pl.ds((head + i) * D, D)] = one.T.astype(jnp.bfloat16)
        cols = pl.ds(head * D, CHUNK * D)
        moves.append(
            pltpu.make_async_copy(out.at[:, cols], out_hbm.at[:, cols], sems.at[head // CHUNK])
        )
        moves[-1].start()
    for move in moves:
        move.wait()


VM = pl.BlockSpec(memory_space=pltpu.VMEM)
SM = pl.BlockSpec(memory_space=pltpu.SMEM)
HB = pl.BlockSpec(memory_space=pltpu.HBM)
LIMIT = 40 * 1024 * 1024
PACK_LIMIT = 60 * 1024 * 1024
PARAMS = pltpu.CompilerParams(vmem_limit_bytes=LIMIT)


def local(queries, keys, values, key_norm_gain, stretch_ids, clean_flags, positions):
    rows, width = keys.shape
    heads = queries.shape[1] // D
    groups, per_group = lax.axis_size("stretch"), lax.axis_size("blk")
    blocks = groups * per_group
    tab = jnp.asarray(rope_tables(rows))
    packed = jax.ShapeDtypeStruct((2 * rows + LABEL_ROWS, width), jnp.bfloat16)
    own = pl.pallas_call(
        pack_kernel,
        out_shape=packed,
        in_specs=[SM] * 3 + [HB] * 4,
        out_specs=VM,
        scratch_shapes=[
            pltpu.VMEM((rows, width), jnp.bfloat16),
            pltpu.VMEM((1, width), jnp.float32),
            pltpu.VMEM(tab.shape, jnp.float32),
            pltpu.SemaphoreType.DMA((4,)),
        ],
        compiler_params=pltpu.CompilerParams(vmem_limit_bytes=PACK_LIMIT),
        cost_estimate=pl.CostEstimate(flops=10**6, bytes_accessed=4 * 10**5, transcendentals=0),
        name="pack",
    )(stretch_ids, clean_flags, positions, keys, values, key_norm_gain[None, :], tab)

    def across(sources):
        pairs = []
        for b in range(blocks):
            column = sources[b % ROW]
            other = b - b % ROW + column + (-ROW if column > b % ROW else ROW)
            if 0 <= other < blocks and other // per_group <= b // per_group:
                pairs.append((other, b))
        return lax.ppermute(own, AXES, pairs)

    c1, c2, c3 = (across(sources) for sources in SOURCES)
    line = [list(range(b, b + ROW)) for b in range(0, blocks, ROW)]
    row = lax.all_gather(own, AXES, axis_index_groups=line)
    rq, stat, mixed = pl.pallas_call(
        first_kernel,
        out_shape=(
            jax.ShapeDtypeStruct((heads * rows, D), jnp.bfloat16),
            jax.ShapeDtypeStruct((8, heads * rows), jnp.float32),
            jax.ShapeDtypeStruct((D, heads * rows), jnp.float32),
        ),
        in_specs=[SM] + [VM] * 4,
        out_specs=(VM,) * 3,
        compiler_params=PARAMS,
        cost_estimate=pl.CostEstimate(
            flops=4 * heads * rows * 4 * rows * D, bytes_accessed=3 * 10**6, transcendentals=10**6
        ),
        name="row",
    )(positions, own, row, queries, tab)
    return pl.pallas_call(
        last_kernel,
        out_shape=jax.ShapeDtypeStruct((rows, heads * D), jnp.bfloat16),
        in_specs=[VM] * 7,
        out_specs=HB,
        scratch_shapes=[
            pltpu.VMEM((rows, heads * D), jnp.bfloat16),
            pltpu.SemaphoreType.DMA((heads // CHUNK,)),
        ],
        compiler_params=PARAMS,
        cost_estimate=pl.CostEstimate(
            flops=4 * heads * rows * 3 * rows * D, bytes_accessed=3 * 10**6, transcendentals=10**6
        ),
        name="across",
    )(c1, c2, c3, own, rq, stat, mixed)


def solution(mesh):
    placed = (
        P(("stretch", "blk"), "head"),
        P(("stretch", "blk"), "head"),
        P(("stretch", "blk"), "head"),
        P("head"),
        P("stretch", "blk"),
        P("stretch", "blk"),
        P("stretch", "blk"),
    )
    return jax.shard_map(
        local, mesh=mesh, in_specs=placed, out_specs=P(("stretch", "blk"), "head"), check_vma=False
    )
```

```python
import functools
import math

import jax
import jax.numpy as jnp
import numpy as np
from jax import lax
from jax.experimental import pallas as pl
from jax.experimental.pallas import tpu as pltpu
from jax.sharding import PartitionSpec as P

D = 128
WINDOW = 3
ROW = WINDOW + 1
SOURCES = ((2, 0, 3, 1), (1, 3, 0, 2), (3, 2, 1, 0))
CHUNK = 2
ROPE_BASE = 10000.0
NEG = -1e30
LABEL_ROWS = 8
AXES = ("stretch", "blk")
SCALE = math.log2(math.e) / math.sqrt(D)


def rope_tables(rows):
    half = D // 2
    f = ROPE_BASE ** (-2.0 * np.arange(half) / D)
    f = np.concatenate([f, f])[None, :]
    t = np.arange(rows, dtype=np.float64)[:, None] * f
    a = 128.0 * np.arange(16, dtype=np.float64)[:, None] * f
    cos = np.concatenate([np.cos(t), np.cos(a)], 0)
    sin = np.concatenate([np.sin(t), np.sin(a)], 0)
    return np.stack([cos, sin]).astype(np.float32)


def angles(pos, tab, rows):
    high = lax.shift_right_logical(pos, 7)
    low = lax.bitwise_and(pos, 127)
    ch, sh = tab[0, pl.ds(rows + high, 1), :], tab[1, pl.ds(rows + high, 1), :]
    cl, sl = tab[0, pl.ds(low, 1), :], tab[1, pl.ds(low, 1), :]
    cp = ch * cl - sh * sl
    sp = sh * cl + ch * sl
    ct, st = tab[0, 0:rows, :], tab[1, 0:rows, :]
    lane = lax.broadcasted_iota(jnp.int32, (1, D), 1)
    sign = jnp.where(lane < D // 2, -1.0, 1.0)
    return cp * ct - sp * st, (sp * ct + cp * st) * sign


def rotate(x, cos, sin):
    return x * cos + pltpu.roll(x, D // 2, 1) * sin


def pack_kernel(
    stretch, clean, pos, k_hbm, v_hbm, gain_hbm, tab_hbm,
    out, k, gain, tab, sems,
):
    rows = k.shape[0]
    moves = [
        pltpu.make_async_copy(src, dst, sems.at[n])
        for n, (src, dst) in enumerate(
            [
                (k_hbm, k),
                (tab_hbm, tab),
                (gain_hbm, gain),
                (v_hbm, out.at[pl.ds(rows, rows)]),
            ]
        )
    ]
    for move in moves:
        move.start()
    for move in moves[:3]:
        move.wait()
    cos, sin = angles(pos[0, 0], tab, rows)
    for g in range(k.shape[1] // D):
        cols = pl.ds(g * D, D)
        x = k[:, cols].astype(jnp.float32)
        x = x * lax.rsqrt(jnp.mean(x * x, axis=-1, keepdims=True) + 1e-6) * gain[:, cols]
        out[0:rows, cols] = rotate(x, cos, sin).astype(jnp.bfloat16)
    for move in moves[3:]:
        move.wait()
    label = stretch[0, 0] + 16 * lax.axis_index("stretch")
    row = lax.broadcasted_iota(jnp.int32, (LABEL_ROWS, k.shape[1]), 0)
    info = jnp.where(row == 0, label, jnp.where(row == 1, clean[0, 0], 1))
    out[pl.ds(2 * rows, LABEL_ROWS), :] = info.astype(jnp.float32).astype(jnp.bfloat16)


def labels(ref):
    top = ref.shape[0] - LABEL_ROWS
    info = ref[pl.ds(top, LABEL_ROWS), 0:D].astype(jnp.float32)
    return info[0:1], info[1:2], info[2:3]


def seen(own, other):
    (stretch, clean, _), (stretch2, clean2, there) = own, other
    earlier = (stretch2 < stretch) & (clean2 > 0.5)
    same = (stretch2 == stretch) & (clean2 == clean)
    return (there > 0.5) & (earlier | same)


def cross(a, b, over_a, over_b):
    return lax.dot_general(
        a, b, (((over_a,), (over_b,)), ((), ())), preferred_element_type=jnp.float32
    )


def blend(q, blocks, bias, g, best):
    cols = pl.ds(g * D, D)
    scores = []
    for kv, hidden in zip(blocks, bias):
        rows = (kv.shape[0] - LABEL_ROWS) // 2
        scores.append(cross(kv[0:rows, cols], q, 1, 1) * SCALE + hidden)
    top = functools.reduce(jnp.maximum, scores)
    top = jnp.max(top, axis=0, keepdims=True)
    best = top if best is None else jnp.maximum(best, top)
    total, mixed = None, None
    for s, kv in zip(scores, blocks):
        rows = (kv.shape[0] - LABEL_ROWS) // 2
        w = jnp.exp2(s - best)
        part = cross(kv[pl.ds(rows, rows), cols], w.astype(jnp.bfloat16), 0, 0)
        total = w if total is None else total + w
        mixed = part if mixed is None else mixed + part
    return best, jnp.sum(total, axis=0, keepdims=True), mixed


def hidden_by(mine, blocks):
    bias = [jnp.where(seen(mine, labels(kv)), 0.0, NEG) for kv in blocks]
    return [jnp.concatenate([b] * CHUNK, axis=1) for b in bias]


def first_kernel(pos, own, row, q, tab, rq, stat_out, mixed_out):
    rows = q.shape[0]
    groups = own.shape[1] // D
    per = q.shape[1] // D // groups
    cos, sin = angles(pos[0, 0], tab, rows)
    blocks = [row.at[i] for i in range(ROW)]
    bias = hidden_by(labels(own), blocks)
    for head in range(0, groups * per, CHUNK):
        turned = [
            rotate(q[:, pl.ds((head + i) * D, D)].astype(jnp.float32), cos, sin)
            for i in range(CHUNK)
        ]
        turned = jnp.concatenate([x.astype(jnp.bfloat16) for x in turned], axis=0)
        rq[pl.ds(head * rows, CHUNK * rows), :] = turned
        best, total, mixed = blend(turned, blocks, bias, head // per, None)
        cols = pl.ds(head * rows, CHUNK * rows)
        stat_out[0:1, cols] = best
        stat_out[1:2, cols] = total
        mixed_out[:, cols] = mixed


def middle_kernel(c1, c2, own, rq, stat, mixed_in, stat_out, mixed_out):
    groups = own.shape[1] // D
    rows = mixed_in.shape[0]
    per = rq.shape[0] // rows // groups
    blocks = (c1, c2)
    bias = hidden_by(labels(own), blocks)
    for head in range(0, groups * per, CHUNK):
        at = pl.ds(head * rows, CHUNK * rows)
        before = stat[0:1, at]
        best, total, mixed = blend(rq[at, :], blocks, bias, head // per, before)
        kept = jnp.exp2(before - best)
        stat_out[0:1, at] = best
        stat_out[1:2, at] = stat[1:2, at] * kept + total
        mixed_out[:, at] = mixed_in[:, at] * kept + mixed


def last_kernel(c3, own, rq, stat, mixed_in, out_hbm, out, sems):
    rows = out.shape[0]
    groups = own.shape[1] // D
    per = rq.shape[0] // rows // groups
    blocks = (c3,)
    bias = hidden_by(labels(own), blocks)
    moves = []
    for head in range(0, groups * per, CHUNK):
        at = pl.ds(head * rows, CHUNK * rows)
        before = stat[0:1, at]
        best, total, mixed = blend(rq[at, :], blocks, bias, head // per, before)
        kept = jnp.exp2(before - best)
        share = 1.0 / (stat[1:2, at] * kept + total)
        mixed = mixed_in[:, at] * (kept * share) + mixed * share
        for i in range(CHUNK):
            one = mixed[:, i * rows : (i + 1) * rows]
            out[:, pl.ds((head + i) * D, D)] = one.T.astype(jnp.bfloat16)
        cols = pl.ds(head * D, CHUNK * D)
        moves.append(
            pltpu.make_async_copy(out.at[:, cols], out_hbm.at[:, cols], sems.at[head // CHUNK])
        )
        moves[-1].start()
    for move in moves:
        move.wait()


VM = pl.BlockSpec(memory_space=pltpu.VMEM)
SM = pl.BlockSpec(memory_space=pltpu.SMEM)
HB = pl.BlockSpec(memory_space=pltpu.HBM)
LIMIT = 40 * 1024 * 1024
PACK_LIMIT = 60 * 1024 * 1024
PARAMS = pltpu.CompilerParams(vmem_limit_bytes=LIMIT)


def local(queries, keys, values, key_norm_gain, stretch_ids, clean_flags, positions):
    rows, width = keys.shape
    heads = queries.shape[1] // D
    groups, per_group = lax.axis_size("stretch"), lax.axis_size("blk")
    blocks = groups * per_group
    tab = jnp.asarray(rope_tables(rows))
    packed = jax.ShapeDtypeStruct((2 * rows + LABEL_ROWS, width), jnp.bfloat16)
    own = pl.pallas_call(
        pack_kernel,
        out_shape=packed,
        in_specs=[SM] * 3 + [HB] * 4,
        out_specs=VM,
        scratch_shapes=[
            pltpu.VMEM((rows, width), jnp.bfloat16),
            pltpu.VMEM((1, width), jnp.float32),
            pltpu.VMEM(tab.shape, jnp.float32),
            pltpu.SemaphoreType.DMA((4,)),
        ],
        compiler_params=pltpu.CompilerParams(vmem_limit_bytes=PACK_LIMIT),
        cost_estimate=pl.CostEstimate(flops=10**6, bytes_accessed=4 * 10**5, transcendentals=0),
        name="pack",
    )(stretch_ids, clean_flags, positions, keys, values, key_norm_gain[None, :], tab)

    def across(sources):
        pairs = []
        for b in range(blocks):
            column = sources[b % ROW]
            other = b - b % ROW + column + (-ROW if column > b % ROW else ROW)
            if 0 <= other < blocks and other // per_group <= b // per_group:
                pairs.append((other, b))
        return lax.ppermute(own, AXES, pairs)

    c1, c2, c3 = (across(sources) for sources in SOURCES)
    line = [list(range(b, b + ROW)) for b in range(0, blocks, ROW)]
    row = lax.all_gather(own, AXES, axis_index_groups=line)
    rq, stat, mixed = pl.pallas_call(
        first_kernel,
        out_shape=(
            jax.ShapeDtypeStruct((heads * rows, D), jnp.bfloat16),
            jax.ShapeDtypeStruct((8, heads * rows), jnp.float32),
            jax.ShapeDtypeStruct((D, heads * rows), jnp.float32),
        ),
        in_specs=[SM] + [VM] * 4,
        out_specs=(VM,) * 3,
        compiler_params=PARAMS,
        cost_estimate=pl.CostEstimate(
            flops=4 * heads * rows * 4 * rows * D, bytes_accessed=3 * 10**6, transcendentals=10**6
        ),
        name="row",
    )(positions, own, row, queries, tab)
    stat, mixed = pl.pallas_call(
        middle_kernel,
        out_shape=(
            jax.ShapeDtypeStruct((8, heads * rows), jnp.float32),
            jax.ShapeDtypeStruct((D, heads * rows), jnp.float32),
        ),
        in_specs=[VM] * 6,
        out_specs=(VM,) * 2,
        compiler_params=PARAMS,
        cost_estimate=pl.CostEstimate(
            flops=4 * heads * rows * 2 * rows * D, bytes_accessed=2 * 10**6, transcendentals=10**6
        ),
        name="across_two",
    )(c1, c2, own, rq, stat, mixed)
    return pl.pallas_call(
        last_kernel,
        out_shape=jax.ShapeDtypeStruct((rows, heads * D), jnp.bfloat16),
        in_specs=[VM] * 5,
        out_specs=HB,
        scratch_shapes=[
            pltpu.VMEM((rows, heads * D), jnp.bfloat16),
            pltpu.SemaphoreType.DMA((heads // CHUNK,)),
        ],
        compiler_params=PARAMS,
        cost_estimate=pl.CostEstimate(
            flops=4 * heads * rows * 3 * rows * D, bytes_accessed=3 * 10**6, transcendentals=10**6
        ),
        name="across_one",
    )(c3, own, rq, stat, mixed)


def solution(mesh):
    placed = (
        P(("stretch", "blk"), "head"),
        P(("stretch", "blk"), "head"),
        P(("stretch", "blk"), "head"),
        P("head"),
        P("stretch", "blk"),
        P("stretch", "blk"),
        P("stretch", "blk"),
    )
    return jax.shard_map(
        local, mesh=mesh, in_specs=placed, out_specs=P(("stretch", "blk"), "head"), check_vma=False
    )
```

```python
import functools
import math

import jax
import jax.numpy as jnp
import numpy as np
from jax import lax
from jax.experimental import pallas as pl
from jax.experimental.pallas import tpu as pltpu
from jax.sharding import PartitionSpec as P

D = 128
WINDOW = 3
ROW = WINDOW + 1
SOURCES = ((1, 3, 0, 2), (2, 0, 3, 1), (3, 2, 1, 0))
CHUNK = 2
ROPE_BASE = 10000.0
NEG = -1e30
LABEL_ROWS = 8
AXES = ("stretch", "blk")
SCALE = math.log2(math.e) / math.sqrt(D)


def rope_tables(rows):
    half = D // 2
    f = ROPE_BASE ** (-2.0 * np.arange(half) / D)
    f = np.concatenate([f, f])[None, :]
    t = np.arange(rows, dtype=np.float64)[:, None] * f
    a = 128.0 * np.arange(16, dtype=np.float64)[:, None] * f
    cos = np.concatenate([np.cos(t), np.cos(a)], 0)
    sin = np.concatenate([np.sin(t), np.sin(a)], 0)
    return np.stack([cos, sin]).astype(np.float32)


def angles(pos, tab, rows):
    high = lax.shift_right_logical(pos, 7)
    low = lax.bitwise_and(pos, 127)
    ch, sh = tab[0, pl.ds(rows + high, 1), :], tab[1, pl.ds(rows + high, 1), :]
    cl, sl = tab[0, pl.ds(low, 1), :], tab[1, pl.ds(low, 1), :]
    cp = ch * cl - sh * sl
    sp = sh * cl + ch * sl
    ct, st = tab[0, 0:rows, :], tab[1, 0:rows, :]
    lane = lax.broadcasted_iota(jnp.int32, (1, D), 1)
    sign = jnp.where(lane < D // 2, -1.0, 1.0)
    return cp * ct - sp * st, (sp * ct + cp * st) * sign


def rotate(x, cos, sin):
    return x * cos + pltpu.roll(x, D // 2, 1) * sin


def pack_kernel(
    stretch, clean, pos, k_hbm, v_hbm, gain_hbm, tab_hbm,
    out, k, gain, tab, sems,
):
    rows = k.shape[0]
    moves = [
        pltpu.make_async_copy(src, dst, sems.at[n])
        for n, (src, dst) in enumerate(
            [
                (k_hbm, k),
                (tab_hbm, tab),
                (gain_hbm, gain),
                (v_hbm, out.at[pl.ds(rows, rows)]),
            ]
        )
    ]
    for move in moves:
        move.start()
    for move in moves[:3]:
        move.wait()
    cos, sin = angles(pos[0, 0], tab, rows)
    for g in range(k.shape[1] // D):
        cols = pl.ds(g * D, D)
        x = k[:, cols].astype(jnp.float32)
        x = x * lax.rsqrt(jnp.mean(x * x, axis=-1, keepdims=True) + 1e-6) * gain[:, cols]
        out[0:rows, cols] = rotate(x, cos, sin).astype(jnp.bfloat16)
    for move in moves[3:]:
        move.wait()
    label = stretch[0, 0] + 16 * lax.axis_index("stretch")
    row = lax.broadcasted_iota(jnp.int32, (LABEL_ROWS, k.shape[1]), 0)
    info = jnp.where(row == 0, label, jnp.where(row == 1, clean[0, 0], 1))
    out[pl.ds(2 * rows, LABEL_ROWS), :] = info.astype(jnp.float32).astype(jnp.bfloat16)


def labels(ref):
    top = ref.shape[0] - LABEL_ROWS
    info = ref[pl.ds(top, LABEL_ROWS), 0:D].astype(jnp.float32)
    return info[0:1], info[1:2], info[2:3]


def seen(own, other):
    (stretch, clean, _), (stretch2, clean2, there) = own, other
    earlier = (stretch2 < stretch) & (clean2 > 0.5)
    same = (stretch2 == stretch) & (clean2 == clean)
    return (there > 0.5) & (earlier | same)


def cross(a, b, over_a, over_b):
    return lax.dot_general(
        a, b, (((over_a,), (over_b,)), ((), ())), preferred_element_type=jnp.float32
    )


def blend(q, blocks, bias, g, best):
    cols = pl.ds(g * D, D)
    scores = []
    for kv, hidden in zip(blocks, bias):
        rows = (kv.shape[0] - LABEL_ROWS) // 2
        scores.append(cross(kv[0:rows, cols], q, 1, 1) * SCALE + hidden)
    top = functools.reduce(jnp.maximum, scores)
    top = jnp.max(top, axis=0, keepdims=True)
    best = top if best is None else jnp.maximum(best, top)
    total, mixed = None, None
    for s, kv in zip(scores, blocks):
        rows = (kv.shape[0] - LABEL_ROWS) // 2
        w = jnp.exp2(s - best)
        part = cross(kv[pl.ds(rows, rows), cols], w.astype(jnp.bfloat16), 0, 0)
        total = w if total is None else total + w
        mixed = part if mixed is None else mixed + part
    return best, jnp.sum(total, axis=0, keepdims=True), mixed


def hidden_by(mine, blocks):
    bias = [jnp.where(seen(mine, labels(kv)), 0.0, NEG) for kv in blocks]
    return [jnp.concatenate([b] * CHUNK, axis=1) for b in bias]


def first_kernel(pos, own, row, q, tab, rq, stat_out, mixed_out):
    rows = q.shape[0]
    groups = own.shape[1] // D
    per = q.shape[1] // D // groups
    cos, sin = angles(pos[0, 0], tab, rows)
    blocks = [row.at[i] for i in range(ROW)]
    bias = hidden_by(labels(own), blocks)
    for head in range(0, groups * per, CHUNK):
        turned = [
            rotate(q[:, pl.ds((head + i) * D, D)].astype(jnp.float32), cos, sin)
            for i in range(CHUNK)
        ]
        turned = jnp.concatenate([x.astype(jnp.bfloat16) for x in turned], axis=0)
        rq[pl.ds(head * rows, CHUNK * rows), :] = turned
        best, total, mixed = blend(turned, blocks, bias, head // per, None)
        cols = pl.ds(head * rows, CHUNK * rows)
        stat_out[0:1, cols] = best
        stat_out[1:2, cols] = total
        mixed_out[:, cols] = mixed


def middle_kernel(c1, c2, own, rq, stat, mixed_in, stat_out, mixed_out):
    groups = own.shape[1] // D
    rows = mixed_in.shape[0]
    per = rq.shape[0] // rows // groups
    blocks = (c1, c2)
    bias = hidden_by(labels(own), blocks)
    for head in range(0, groups * per, CHUNK):
        at = pl.ds(head * rows, CHUNK * rows)
        before = stat[0:1, at]
        best, total, mixed = blend(rq[at, :], blocks, bias, head // per, before)
        kept = jnp.exp2(before - best)
        stat_out[0:1, at] = best
        stat_out[1:2, at] = stat[1:2, at] * kept + total
        mixed_out[:, at] = mixed_in[:, at] * kept + mixed


def last_kernel(c3, own, rq, stat, mixed_in, out_hbm, out, sems):
    rows = out.shape[0]
    groups = own.shape[1] // D
    per = rq.shape[0] // rows // groups
    blocks = (c3,)
    bias = hidden_by(labels(own), blocks)
    moves = []
    for head in range(0, groups * per, CHUNK):
        at = pl.ds(head * rows, CHUNK * rows)
        before = stat[0:1, at]
        best, total, mixed = blend(rq[at, :], blocks, bias, head // per, before)
        kept = jnp.exp2(before - best)
        share = 1.0 / (stat[1:2, at] * kept + total)
        mixed = mixed_in[:, at] * (kept * share) + mixed * share
        for i in range(CHUNK):
            one = mixed[:, i * rows : (i + 1) * rows]
            out[:, pl.ds((head + i) * D, D)] = one.T.astype(jnp.bfloat16)
        cols = pl.ds(head * D, CHUNK * D)
        moves.append(
            pltpu.make_async_copy(out.at[:, cols], out_hbm.at[:, cols], sems.at[head // CHUNK])
        )
        moves[-1].start()
    for move in moves:
        move.wait()


VM = pl.BlockSpec(memory_space=pltpu.VMEM)
SM = pl.BlockSpec(memory_space=pltpu.SMEM)
HB = pl.BlockSpec(memory_space=pltpu.HBM)
LIMIT = 40 * 1024 * 1024
PACK_LIMIT = 60 * 1024 * 1024
PARAMS = pltpu.CompilerParams(vmem_limit_bytes=LIMIT)


def local(queries, keys, values, key_norm_gain, stretch_ids, clean_flags, positions):
    rows, width = keys.shape
    heads = queries.shape[1] // D
    groups, per_group = lax.axis_size("stretch"), lax.axis_size("blk")
    blocks = groups * per_group
    tab = jnp.asarray(rope_tables(rows))
    packed = jax.ShapeDtypeStruct((2 * rows + LABEL_ROWS, width), jnp.bfloat16)
    own = pl.pallas_call(
        pack_kernel,
        out_shape=packed,
        in_specs=[SM] * 3 + [HB] * 4,
        out_specs=VM,
        scratch_shapes=[
            pltpu.VMEM((rows, width), jnp.bfloat16),
            pltpu.VMEM((1, width), jnp.float32),
            pltpu.VMEM(tab.shape, jnp.float32),
            pltpu.SemaphoreType.DMA((4,)),
        ],
        compiler_params=pltpu.CompilerParams(vmem_limit_bytes=PACK_LIMIT),
        cost_estimate=pl.CostEstimate(flops=10**6, bytes_accessed=4 * 10**5, transcendentals=0),
        name="pack",
    )(stretch_ids, clean_flags, positions, keys, values, key_norm_gain[None, :], tab)

    def across(sources):
        pairs = []
        for b in range(blocks):
            column = sources[b % ROW]
            other = b - b % ROW + column + (-ROW if column > b % ROW else ROW)
            if 0 <= other < blocks and other // per_group <= b // per_group:
                pairs.append((other, b))
        return lax.ppermute(own, AXES, pairs)

    c1, c2, c3 = (across(sources) for sources in SOURCES)
    line = [list(range(b, b + ROW)) for b in range(0, blocks, ROW)]
    row = lax.all_gather(own, AXES, axis_index_groups=line)
    rq, stat, mixed = pl.pallas_call(
        first_kernel,
        out_shape=(
            jax.ShapeDtypeStruct((heads * rows, D), jnp.bfloat16),
            jax.ShapeDtypeStruct((8, heads * rows), jnp.float32),
            jax.ShapeDtypeStruct((D, heads * rows), jnp.float32),
        ),
        in_specs=[SM] + [VM] * 4,
        out_specs=(VM,) * 3,
        compiler_params=PARAMS,
        cost_estimate=pl.CostEstimate(
            flops=4 * heads * rows * 4 * rows * D, bytes_accessed=3 * 10**6, transcendentals=10**6
        ),
        name="row",
    )(positions, own, row, queries, tab)
    stat, mixed = pl.pallas_call(
        middle_kernel,
        out_shape=(
            jax.ShapeDtypeStruct((8, heads * rows), jnp.float32),
            jax.ShapeDtypeStruct((D, heads * rows), jnp.float32),
        ),
        in_specs=[VM] * 6,
        out_specs=(VM,) * 2,
        compiler_params=PARAMS,
        cost_estimate=pl.CostEstimate(
            flops=4 * heads * rows * 2 * rows * D, bytes_accessed=2 * 10**6, transcendentals=10**6
        ),
        name="across_two",
    )(c1, c2, own, rq, stat, mixed)
    return pl.pallas_call(
        last_kernel,
        out_shape=jax.ShapeDtypeStruct((rows, heads * D), jnp.bfloat16),
        in_specs=[VM] * 5,
        out_specs=HB,
        scratch_shapes=[
            pltpu.VMEM((rows, heads * D), jnp.bfloat16),
            pltpu.SemaphoreType.DMA((heads // CHUNK,)),
        ],
        compiler_params=PARAMS,
        cost_estimate=pl.CostEstimate(
            flops=4 * heads * rows * 3 * rows * D, bytes_accessed=3 * 10**6, transcendentals=10**6
        ),
        name="across_one",
    )(c3, own, rq, stat, mixed)


def solution(mesh):
    placed = (
        P(("stretch", "blk"), "head"),
        P(("stretch", "blk"), "head"),
        P(("stretch", "blk"), "head"),
        P("head"),
        P("stretch", "blk"),
        P("stretch", "blk"),
        P("stretch", "blk"),
    )
    return jax.shard_map(
        local, mesh=mesh, in_specs=placed, out_specs=P(("stretch", "blk"), "head"), check_vma=False
    )
```

```python
import functools
import math

import jax
import jax.numpy as jnp
import numpy as np
from jax import lax
from jax.experimental import pallas as pl
from jax.experimental.pallas import tpu as pltpu
from jax.sharding import PartitionSpec as P

D = 128
WINDOW = 3
ROW = WINDOW + 1
SOURCES = ((1, 3, 0, 2), (2, 0, 3, 1), (3, 2, 1, 0))
CHUNK = 2
ROPE_BASE = 10000.0
NEG = -1e30
LABEL_ROWS = 8
AXES = ("stretch", "blk")
SCALE = math.log2(math.e) / math.sqrt(D)


def rope_tables(rows):
    half = D // 2
    f = ROPE_BASE ** (-2.0 * np.arange(half) / D)
    f = np.concatenate([f, f])[None, :]
    t = np.arange(rows, dtype=np.float64)[:, None] * f
    a = 128.0 * np.arange(16, dtype=np.float64)[:, None] * f
    cos = np.concatenate([np.cos(t), np.cos(a)], 0)
    sin = np.concatenate([np.sin(t), np.sin(a)], 0)
    return np.stack([cos, sin]).astype(np.float32)


def angles(pos, tab, rows):
    high = lax.shift_right_logical(pos, 7)
    low = lax.bitwise_and(pos, 127)
    ch, sh = tab[0, pl.ds(rows + high, 1), :], tab[1, pl.ds(rows + high, 1), :]
    cl, sl = tab[0, pl.ds(low, 1), :], tab[1, pl.ds(low, 1), :]
    cp = ch * cl - sh * sl
    sp = sh * cl + ch * sl
    ct, st = tab[0, 0:rows, :], tab[1, 0:rows, :]
    lane = lax.broadcasted_iota(jnp.int32, (1, D), 1)
    sign = jnp.where(lane < D // 2, -1.0, 1.0)
    return cp * ct - sp * st, (sp * ct + cp * st) * sign


def rotate(x, cos, sin):
    return x * cos + pltpu.roll(x, D // 2, 1) * sin


def pack_kernel(
    stretch, clean, pos, k_hbm, v_hbm, gain_hbm, tab_hbm,
    out, k, gain, tab, sems,
):
    rows = k.shape[0]
    moves = [
        pltpu.make_async_copy(src, dst, sems.at[n])
        for n, (src, dst) in enumerate(
            [
                (k_hbm, k),
                (tab_hbm, tab),
                (gain_hbm, gain),
                (v_hbm, out.at[pl.ds(rows, rows)]),
            ]
        )
    ]
    for move in moves:
        move.start()
    for move in moves[:3]:
        move.wait()
    cos, sin = angles(pos[0, 0], tab, rows)
    for g in range(k.shape[1] // D):
        cols = pl.ds(g * D, D)
        x = k[:, cols].astype(jnp.float32)
        x = x * lax.rsqrt(jnp.mean(x * x, axis=-1, keepdims=True) + 1e-6) * gain[:, cols]
        out[0:rows, cols] = rotate(x, cos, sin).astype(jnp.bfloat16)
    for move in moves[3:]:
        move.wait()
    label = stretch[0, 0] + 16 * lax.axis_index("stretch")
    row = lax.broadcasted_iota(jnp.int32, (LABEL_ROWS, k.shape[1]), 0)
    info = jnp.where(row == 0, label, jnp.where(row == 1, clean[0, 0], 1))
    out[pl.ds(2 * rows, LABEL_ROWS), :] = info.astype(jnp.float32).astype(jnp.bfloat16)


def labels(ref):
    top = ref.shape[0] - LABEL_ROWS
    info = ref[pl.ds(top, LABEL_ROWS), 0:D].astype(jnp.float32)
    return info[0:1], info[1:2], info[2:3]


def seen(own, other):
    (stretch, clean, _), (stretch2, clean2, there) = own, other
    earlier = (stretch2 < stretch) & (clean2 > 0.5)
    same = (stretch2 == stretch) & (clean2 == clean)
    return (there > 0.5) & (earlier | same)


def cross(a, b, over_a, over_b):
    return lax.dot_general(
        a, b, (((over_a,), (over_b,)), ((), ())), preferred_element_type=jnp.float32
    )


def blend(q, blocks, bias, g, best):
    cols = pl.ds(g * D, D)
    scores = []
    for kv, hidden in zip(blocks, bias):
        rows = (kv.shape[0] - LABEL_ROWS) // 2
        scores.append(cross(kv[0:rows, cols], q, 1, 1) * SCALE + hidden)
    top = functools.reduce(jnp.maximum, scores)
    top = jnp.max(top, axis=0, keepdims=True)
    best = top if best is None else jnp.maximum(best, top)
    total, mixed = None, None
    for s, kv in zip(scores, blocks):
        rows = (kv.shape[0] - LABEL_ROWS) // 2
        w = jnp.exp2(s - best)
        part = cross(kv[pl.ds(rows, rows), cols], w.astype(jnp.bfloat16), 0, 0)
        total = w if total is None else total + w
        mixed = part if mixed is None else mixed + part
    return best, jnp.sum(total, axis=0, keepdims=True), mixed


def hidden_by(mine, blocks):
    bias = [jnp.where(seen(mine, labels(kv)), 0.0, NEG) for kv in blocks]
    return [jnp.concatenate([b] * CHUNK, axis=1) for b in bias]


def first_kernel(pos, own, row, q, tab, rq, stat_out, mixed_out):
    rows = q.shape[0]
    groups = own.shape[1] // D
    per = q.shape[1] // D // groups
    cos, sin = angles(pos[0, 0], tab, rows)
    blocks = [row.at[i] for i in range(ROW)]
    bias = hidden_by(labels(own), blocks)
    for head in range(0, groups * per, CHUNK):
        turned = [
            rotate(q[:, pl.ds((head + i) * D, D)].astype(jnp.float32), cos, sin)
            for i in range(CHUNK)
        ]
        turned = jnp.concatenate([x.astype(jnp.bfloat16) for x in turned], axis=0)
        rq[pl.ds(head * rows, CHUNK * rows), :] = turned
        best, total, mixed = blend(turned, blocks, bias, head // per, None)
        cols = pl.ds(head * rows, CHUNK * rows)
        stat_out[0:1, cols] = best
        stat_out[1:2, cols] = total
        mixed_out[:, cols] = mixed


def middle_kernel(c1, own, rq, stat, mixed_in, stat_out, mixed_out):
    groups = own.shape[1] // D
    rows = mixed_in.shape[0]
    per = rq.shape[0] // rows // groups
    blocks = (c1,)
    bias = hidden_by(labels(own), blocks)
    for head in range(0, groups * per, CHUNK):
        at = pl.ds(head * rows, CHUNK * rows)
        before = stat[0:1, at]
        best, total, mixed = blend(rq[at, :], blocks, bias, head // per, before)
        kept = jnp.exp2(before - best)
        stat_out[0:1, at] = best
        stat_out[1:2, at] = stat[1:2, at] * kept + total
        mixed_out[:, at] = mixed_in[:, at] * kept + mixed


def last_kernel(c2, c3, own, rq, stat, mixed_in, out_hbm, out, sems):
    rows = out.shape[0]
    groups = own.shape[1] // D
    per = rq.shape[0] // rows // groups
    blocks = (c2, c3)
    bias = hidden_by(labels(own), blocks)
    moves = []
    for head in range(0, groups * per, CHUNK):
        at = pl.ds(head * rows, CHUNK * rows)
        before = stat[0:1, at]
        best, total, mixed = blend(rq[at, :], blocks, bias, head // per, before)
        kept = jnp.exp2(before - best)
        share = 1.0 / (stat[1:2, at] * kept + total)
        mixed = mixed_in[:, at] * (kept * share) + mixed * share
        for i in range(CHUNK):
            one = mixed[:, i * rows : (i + 1) * rows]
            out[:, pl.ds((head + i) * D, D)] = one.T.astype(jnp.bfloat16)
        cols = pl.ds(head * D, CHUNK * D)
        moves.append(
            pltpu.make_async_copy(out.at[:, cols], out_hbm.at[:, cols], sems.at[head // CHUNK])
        )
        moves[-1].start()
    for move in moves:
        move.wait()


VM = pl.BlockSpec(memory_space=pltpu.VMEM)
SM = pl.BlockSpec(memory_space=pltpu.SMEM)
HB = pl.BlockSpec(memory_space=pltpu.HBM)
LIMIT = 40 * 1024 * 1024
PACK_LIMIT = 60 * 1024 * 1024
PARAMS = pltpu.CompilerParams(vmem_limit_bytes=LIMIT)


def local(queries, keys, values, key_norm_gain, stretch_ids, clean_flags, positions):
    rows, width = keys.shape
    heads = queries.shape[1] // D
    groups, per_group = lax.axis_size("stretch"), lax.axis_size("blk")
    blocks = groups * per_group
    tab = jnp.asarray(rope_tables(rows))
    packed = jax.ShapeDtypeStruct((2 * rows + LABEL_ROWS, width), jnp.bfloat16)
    own = pl.pallas_call(
        pack_kernel,
        out_shape=packed,
        in_specs=[SM] * 3 + [HB] * 4,
        out_specs=VM,
        scratch_shapes=[
            pltpu.VMEM((rows, width), jnp.bfloat16),
            pltpu.VMEM((1, width), jnp.float32),
            pltpu.VMEM(tab.shape, jnp.float32),
            pltpu.SemaphoreType.DMA((4,)),
        ],
        compiler_params=pltpu.CompilerParams(vmem_limit_bytes=PACK_LIMIT),
        cost_estimate=pl.CostEstimate(flops=10**6, bytes_accessed=4 * 10**5, transcendentals=0),
        name="pack",
    )(stretch_ids, clean_flags, positions, keys, values, key_norm_gain[None, :], tab)

    def across(sources):
        pairs = []
        for b in range(blocks):
            column = sources[b % ROW]
            other = b - b % ROW + column + (-ROW if column > b % ROW else ROW)
            if 0 <= other < blocks and other // per_group <= b // per_group:
                pairs.append((other, b))
        return lax.ppermute(own, AXES, pairs)

    c1, c2, c3 = (across(sources) for sources in SOURCES)
    line = [list(range(b, b + ROW)) for b in range(0, blocks, ROW)]
    row = lax.all_gather(own, AXES, axis_index_groups=line)
    rq, stat, mixed = pl.pallas_call(
        first_kernel,
        out_shape=(
            jax.ShapeDtypeStruct((heads * rows, D), jnp.bfloat16),
            jax.ShapeDtypeStruct((8, heads * rows), jnp.float32),
            jax.ShapeDtypeStruct((D, heads * rows), jnp.float32),
        ),
        in_specs=[SM] + [VM] * 4,
        out_specs=(VM,) * 3,
        compiler_params=PARAMS,
        cost_estimate=pl.CostEstimate(
            flops=4 * heads * rows * 4 * rows * D, bytes_accessed=3 * 10**6, transcendentals=10**6
        ),
        name="row",
    )(positions, own, row, queries, tab)
    stat, mixed = pl.pallas_call(
        middle_kernel,
        out_shape=(
            jax.ShapeDtypeStruct((8, heads * rows), jnp.float32),
            jax.ShapeDtypeStruct((D, heads * rows), jnp.float32),
        ),
        in_specs=[VM] * 5,
        out_specs=(VM,) * 2,
        compiler_params=PARAMS,
        cost_estimate=pl.CostEstimate(
            flops=4 * heads * rows * rows * D, bytes_accessed=2 * 10**6, transcendentals=10**6
        ),
        name="across_first",
    )(c1, own, rq, stat, mixed)
    return pl.pallas_call(
        last_kernel,
        out_shape=jax.ShapeDtypeStruct((rows, heads * D), jnp.bfloat16),
        in_specs=[VM] * 6,
        out_specs=HB,
        scratch_shapes=[
            pltpu.VMEM((rows, heads * D), jnp.bfloat16),
            pltpu.SemaphoreType.DMA((heads // CHUNK,)),
        ],
        compiler_params=PARAMS,
        cost_estimate=pl.CostEstimate(
            flops=4 * heads * rows * 2 * rows * D, bytes_accessed=3 * 10**6, transcendentals=10**6
        ),
        name="across_rest",
    )(c2, c3, own, rq, stat, mixed)


def solution(mesh):
    placed = (
        P(("stretch", "blk"), "head"),
        P(("stretch", "blk"), "head"),
        P(("stretch", "blk"), "head"),
        P("head"),
        P("stretch", "blk"),
        P("stretch", "blk"),
        P("stretch", "blk"),
    )
    return jax.shard_map(
        local, mesh=mesh, in_specs=placed, out_specs=P(("stretch", "blk"), "head"), check_vma=False
    )
```
